32 devices in a mesh: rep: 16 (over z, y, core), shard: 2 (over x).
Axes of the slice: x: 2, y: 2, z: 4, core: 2. Of those that a mesh axis runs over, the one named last changes fastest.
Arguments:
- tokens: bfloat16 [4096, 1024], P(('rep', 'shard')), may hold values from -6 to 6
- lengths: int32 [32], P(('rep', 'shard')), may hold values from 16 to 128, as said below
- cotangent: bfloat16 [4096, 1024], P(('rep', 'shard')), may hold values from -6 to 6
- qkv_weight: bfloat16 [1024, 3072], P('shard'), may hold values from -0.1875 to 0.1875
- query_bias: bfloat16 [1024], P('shard'), may hold values from -3 to 3
- value_bias: bfloat16 [1024], P('shard'), may hold values from -3 to 3
- out_weight: bfloat16 [1024, 1024], P('shard'), may hold values from -0.75 to 0.75
- out_bias: bfloat16 [1024], P('shard'), may hold values from -3 to 3
- norm1_gain: bfloat16 [1024], P('shard'), may hold values from 0.5 to 1.5
- norm1_bias: bfloat16 [1024], P('shard'), may hold values from -3 to 3
- up_weight: bfloat16 [1024, 4096], P('shard'), may hold values from -0.1875 to 0.1875
- up_bias: bfloat16 [4096], P('shard'), may hold values from -3 to 3
- down_weight: bfloat16 [4096, 1024], P('shard'), may hold values from -0.09375 to 0.09375
- down_bias: bfloat16 [1024], P('shard'), may hold values from -3 to 3
- norm2_gain: bfloat16 [1024], P('shard'), may hold values from 0.5 to 1.5
- norm2_bias: bfloat16 [1024], P('shard'), may hold values from -3 to 3
Outputs:
- layer_out: bfloat16 [4096, 1024], P(('rep', 'shard'))
- input_grad: bfloat16 [4096, 1024], P(('rep', 'shard'))
- qkv_weight_grad: float32 [1024, 3072], P('shard')
- query_bias_grad: float32 [1024], P('shard')
- value_bias_grad: float32 [1024], P('shard')
- out_weight_grad: float32 [1024, 1024], P('shard')
- out_bias_grad: float32 [1024], P('shard')
- norm1_gain_grad: float32 [1024], P('shard')
- norm1_bias_grad: float32 [1024], P('shard')
- up_weight_grad: float32 [1024, 4096], P('shard')
- up_bias_grad: float32 [4096], P('shard')
- down_weight_grad: float32 [4096, 1024], P('shard')
- down_bias_grad: float32 [1024], P('shard')
- norm2_gain_grad: float32 [1024], P('shard')
- norm2_bias_grad: float32 [1024], P('shard')
The draws below stay inside these ranges and needn't reach their ends.
Inputs may be any that keep to these rules, and one draw needn't show every extreme that they name: The alive slots of a sequence are its first lengths slots; some sequence has all 128 alive and some only 16.
All inputs are finite; a program needn't handle non-finite values.
Results may differ from the reference program's by a relative error of at most 0.018.
Values may be sent and summed in bfloat16 or wider, within the bound.
No kernel may reach another device: no remote copies, remote signals or barrier semaphores. Data moves between devices by JAX's collectives and lax.ppermute only.
A program may use at most 192 MiB of HBM per device.

```python
import math
import jax
import jax.numpy as jnp
from jax import lax

D = 1024
HEADS = 16
FF = 4096
LEN = 128
SEQS = 32
TOKENS = 4096


def draw_lengths(key, part):
    values = jax.random.randint(key, (SEQS,), LEN // 8, LEN + 1)
    places = jnp.arange(SEQS)
    values = jnp.where(places == 0, LEN, values)
    values = jnp.where(places == SEQS - 1, LEN // 8, values)
    return values.astype(jnp.int32)


def shard_levels(rng, extent, split, least, largest):
    def one(axis_at, parts):
        heights = jax.random.uniform(jax.random.fold_in(jax.random.fold_in(rng, 6), axis_at), (parts,), jnp.float32, least / len(split), largest / len(split))
        return jnp.repeat(jnp.exp(heights), extent[axis_at] // parts).reshape((-1,) + (1,) * (len(extent) - axis_at - 1))

    gain = one(*split[0])
    for cut in split[1:]:
        gain = gain * one(*cut)
    return gain


def gaussian(stream_key, shape, deviation, bound, cuts=(), held_as=jnp.bfloat16):
    loudness = shard_levels(stream_key, shape, cuts, -0.22, 0.18) if cuts else 1.0
    result = jax.random.normal(stream_key, shape, jnp.float32) * deviation * loudness
    return jnp.minimum(jnp.maximum(result, -bound), bound).astype(held_as)


def setup_inputs(seed: int = 0) -> dict:
    keys = jax.random.split(jax.random.key(seed), 17)
    tokens = gaussian(keys[0], (TOKENS, D), 1.0, 6.0, ((0, 32),))
    lengths = draw_lengths(jax.random.fold_in(keys[16], 71), 0)
    cotangent = gaussian(keys[2], (TOKENS, D), 1.0, 6.0, ((0, 32),))
    qkv_weight = gaussian(keys[3], (D, 3 * D), D ** -0.5, 0.1875, ((0, 2),))
    query_bias = gaussian(keys[4], (D,), 0.5, 3.0, ((0, 2),))
    value_bias = gaussian(keys[5], (D,), 0.5, 3.0, ((0, 2),))
    out_weight = gaussian(keys[6], (D, D), (D // 16) ** -0.5, 0.75, ((0, 2),))
    out_bias = gaussian(keys[7], (D,), 0.5, 3.0, ((0, 2),))
    norm1_gain = jnp.clip(1.0 + 0.1 * jax.random.normal(keys[8], (D,), jnp.float32), 0.5, 1.5).astype(jnp.bfloat16)
    norm1_bias = gaussian(keys[9], (D,), 0.5, 3.0, ((0, 2),))
    up_weight = gaussian(keys[10], (D, FF), D ** -0.5, 0.1875, ((0, 2),))
    up_bias = gaussian(keys[11], (FF,), 0.5, 3.0, ((0, 2),))
    down_weight = gaussian(keys[12], (FF, D), FF ** -0.5, 0.09375, ((0, 2),))
    down_bias = gaussian(keys[13], (D,), 0.5, 3.0, ((0, 2),))
    norm2_gain = jnp.clip(1.0 + 0.1 * jax.random.normal(keys[14], (D,), jnp.float32), 0.5, 1.5).astype(jnp.bfloat16)
    norm2_bias = gaussian(keys[15], (D,), 0.5, 3.0, ((0, 2),))
    return dict(tokens=tokens, lengths=lengths, cotangent=cotangent, qkv_weight=qkv_weight, query_bias=query_bias, value_bias=value_bias, out_weight=out_weight, out_bias=out_bias, norm1_gain=norm1_gain, norm1_bias=norm1_bias, up_weight=up_weight, up_bias=up_bias, down_weight=down_weight, down_bias=down_bias, norm2_gain=norm2_gain, norm2_bias=norm2_bias)


EPS = 1e-06
ROOT_HALF = 0.7071067811865476
INV_ROOT_TAU = 0.3989422804014327

def erf_gelu(inputs):
    return 0.5 * inputs * (1.0 + jax.scipy.special.erf(inputs * ROOT_HALF))

def gelu_slope(inputs):
    cumul = 0.5 * (1.0 + jax.scipy.special.erf(inputs * ROOT_HALF))
    return cumul + inputs * jnp.exp(-0.5 * inputs * inputs) * INV_ROOT_TAU

def norm_rows(rows_in, norm_gain, norm_shift):
    row_mean = lax.optimization_barrier(jnp.mean(rows_in, axis=-1, keepdims=True))
    centred = rows_in - row_mean
    variance = lax.optimization_barrier(jnp.mean(centred * centred, axis=-1, keepdims=True))
    inv_std = lax.rsqrt(variance + EPS)
    normed = centred * inv_std
    return (normed * norm_gain + norm_shift, normed, inv_std)

def norm_back(upstream, normed, inv_std, norm_gain):
    scaled = upstream * norm_gain
    mean_scaled = lax.optimization_barrier(jnp.mean(scaled, axis=-1, keepdims=True))
    mean_proj = lax.optimization_barrier(jnp.mean(scaled * normed, axis=-1, keepdims=True))
    return inv_std * (scaled - mean_scaled - normed * mean_proj)

def split_heads(qkv_rows, lengths):
    num_seqs = lengths.shape[0]
    seq_span = qkv_rows.shape[0] // num_seqs
    head_size = qkv_rows.shape[1] // (3 * HEADS)
    shaped = qkv_rows.reshape(num_seqs, seq_span, 3, HEADS, head_size).astype(jnp.float32)
    alive = (jnp.arange(seq_span, dtype=jnp.int32)[None, :] < lengths[:, None]).astype(jnp.float32)
    return (shaped[:, :, 0], shaped[:, :, 1], shaped[:, :, 2], alive[:, None, None, :], head_size)

def attn_probs_of(queries, keys_part, alive, head_size):
    score_scale = head_size ** (-0.5)
    scores = jnp.einsum('sqhd,skhd->shqk', queries, keys_part) * score_scale
    log_total = jnp.log(lax.optimization_barrier(jnp.sum(jnp.exp(scores) * alive, axis=-1, keepdims=True)))
    return jnp.exp(scores - log_total) * alive

def dot_rows(left, right):
    return jnp.dot(left.T, right, preferred_element_type=jnp.float32)

def dot_cols(left, right):
    return jnp.dot(left, right.T, preferred_element_type=jnp.float32)

def layer_block(tokens, lengths, cotangent, weights_all):
    qkv_weight, query_bias, value_bias, out_weight, out_bias, norm1_gain, norm1_bias, up_weight, up_bias, down_weight, down_bias, norm2_gain, norm2_bias = weights_all
    f32 = jnp.float32
    bf16 = jnp.bfloat16
    rows = tokens.shape[0]
    width = tokens.shape[1]
    qkv_bias = jnp.concatenate([query_bias, jnp.zeros_like(query_bias), value_bias]).astype(f32)
    qkv_rows = (jnp.dot(tokens, qkv_weight, preferred_element_type=f32) + qkv_bias).astype(bf16)
    queries, keys_part, values_part, alive, head_size = split_heads(qkv_rows, lengths)
    probs_full = attn_probs_of(queries, keys_part, alive, head_size)
    probs_half = probs_full.astype(bf16).astype(f32)
    context = jnp.einsum('shqk,skhd->sqhd', probs_half, values_part).reshape(rows, width).astype(bf16)
    gain1 = norm1_gain.astype(f32)
    resid1 = tokens.astype(f32) + jnp.dot(context, out_weight, preferred_element_type=f32) + out_bias.astype(f32)
    hidden1, normed1, inv_std1 = norm_rows(resid1, gain1, norm1_bias.astype(f32))
    hidden1_half = hidden1.astype(bf16)
    pre_act = jnp.dot(hidden1_half, up_weight, preferred_element_type=f32) + up_bias.astype(f32)
    activ_half = erf_gelu(pre_act).astype(bf16)
    gain2 = norm2_gain.astype(f32)
    resid2 = hidden1 + jnp.dot(activ_half, down_weight, preferred_element_type=f32) + down_bias.astype(f32)
    layer_f32, normed2, inv_std2 = norm_rows(resid2, gain2, norm2_bias.astype(f32))
    layer_out = layer_f32.astype(bf16)
    upstream = cotangent.astype(f32)
    grad_gain2 = lax.optimization_barrier(jnp.sum(upstream * normed2, axis=0))
    grad_shift2 = lax.optimization_barrier(jnp.sum(upstream, axis=0))
    grad_resid2 = norm_back(upstream, normed2, inv_std2, gain2)
    grad_mlp_half = grad_resid2.astype(bf16)
    grad_down = dot_rows(activ_half, grad_mlp_half)
    grad_down_bias = lax.optimization_barrier(jnp.sum(grad_resid2, axis=0))
    grad_pre = dot_cols(grad_mlp_half, down_weight) * gelu_slope(pre_act)
    grad_pre_half = grad_pre.astype(bf16)
    grad_up = dot_rows(hidden1_half, grad_pre_half)
    grad_up_bias = lax.optimization_barrier(jnp.sum(grad_pre, axis=0))
    grad_hidden1 = grad_resid2 + dot_cols(grad_pre_half, up_weight)
    grad_gain1 = lax.optimization_barrier(jnp.sum(grad_hidden1 * normed1, axis=0))
    grad_shift1 = lax.optimization_barrier(jnp.sum(grad_hidden1, axis=0))
    grad_resid1 = norm_back(grad_hidden1, normed1, inv_std1, gain1)
    grad_attn_half = grad_resid1.astype(bf16)
    grad_out = dot_rows(context, grad_attn_half)
    grad_out_bias = lax.optimization_barrier(jnp.sum(grad_resid1, axis=0))
    grad_context = dot_cols(grad_attn_half, out_weight).astype(bf16)
    grad_heads = grad_context.astype(f32).reshape(queries.shape)
    grad_values = jnp.einsum('shqk,sqhd->skhd', probs_half, grad_heads)
    grad_probs = jnp.einsum('sqhd,skhd->shqk', grad_heads, values_part)
    grad_scores = probs_full * (grad_probs - lax.optimization_barrier(jnp.sum(probs_full * grad_probs, axis=-1, keepdims=True))) * head_size ** (-0.5)
    grad_scores_half = grad_scores.astype(bf16).astype(f32)
    grad_queries = jnp.einsum('shqk,skhd->sqhd', grad_scores_half, keys_part)
    grad_keys = jnp.einsum('shqk,sqhd->skhd', grad_scores_half, queries)
    grad_qkv = jnp.concatenate([grad_queries.reshape(rows, width), grad_keys.reshape(rows, width), grad_values.reshape(rows, width)], axis=1)
    grad_qkv_half = grad_qkv.astype(bf16)
    grad_qkv_weight = dot_rows(tokens, grad_qkv_half)
    grad_query_bias = lax.optimization_barrier(jnp.sum(grad_qkv[:, :width], axis=0))
    grad_value_bias = lax.optimization_barrier(jnp.sum(grad_qkv[:, 2 * width:], axis=0))
    input_grad = (grad_resid1 + dot_cols(grad_qkv_half, qkv_weight)).astype(bf16)
    grads = (grad_qkv_weight, grad_query_bias, grad_value_bias, grad_out, grad_out_bias, grad_gain1, grad_shift1, grad_up, grad_up_bias, grad_down, grad_down_bias, grad_gain2, grad_shift2)
    return (layer_out, input_grad, grads)

def reference(tokens, lengths, cotangent, qkv_weight, query_bias, value_bias, out_weight, out_bias, norm1_gain, norm1_bias, up_weight, up_bias, down_weight, down_bias, norm2_gain, norm2_bias):
    weights_all = (qkv_weight, query_bias, value_bias, out_weight, out_bias, norm1_gain, norm1_bias, up_weight, up_bias, down_weight, down_bias, norm2_gain, norm2_bias)
    group = math.gcd(SEQS, max(1, 4096 // LEN))
    blocks = SEQS // group
    token_blocks = tokens.reshape(blocks, group * LEN, D)
    cot_blocks = cotangent.reshape(blocks, group * LEN, D)
    length_blocks = lengths.reshape(blocks, group)
    zeros_init = tuple((jnp.zeros(item.shape, jnp.float32) for item in weights_all))

    def one_block(carry, inputs_now):
        token_now, length_now, cot_now = inputs_now
        layer_out, input_grad, grads = layer_block(token_now, length_now, cot_now, weights_all)
        carry = tuple((total + part for total, part in zip(carry, grads)))
        return (carry, (layer_out, input_grad))
    totals, (outs_all, grads_in) = lax.scan(one_block, zeros_init, (token_blocks, length_blocks, cot_blocks))
    layer_out = outs_all.reshape(TOKENS, D)
    input_grad = grads_in.reshape(TOKENS, D)
    return (layer_out, input_grad, totals[0], totals[1], totals[2], totals[3], totals[4], totals[5], totals[6], totals[7], totals[8], totals[9], totals[10], totals[11], totals[12])
```

```python
import jax
import jax.numpy as jnp
from jax import lax
from jax.sharding import PartitionSpec as P

HEADS = 16
CORES = 2

EPS = 1e-06
ROOT_HALF = 0.7071067811865476
INV_ROOT_TAU = 0.3989422804014327

F32 = jnp.float32
BF16 = jnp.bfloat16


def erf_gelu(inputs):
    return 0.5 * inputs * (1.0 + jax.scipy.special.erf(inputs * ROOT_HALF))


def gelu_slope(inputs):
    cumul = 0.5 * (1.0 + jax.scipy.special.erf(inputs * ROOT_HALF))
    return cumul + inputs * jnp.exp(-0.5 * inputs * inputs) * INV_ROOT_TAU


def norm_rows(rows_in, norm_gain, norm_shift):
    row_mean = jnp.mean(rows_in, axis=-1, keepdims=True)
    centred = rows_in - row_mean
    variance = jnp.mean(centred * centred, axis=-1, keepdims=True)
    inv_std = lax.rsqrt(variance + EPS)
    normed = centred * inv_std
    return (normed * norm_gain + norm_shift, normed, inv_std)


def norm_back(upstream, normed, inv_std, norm_gain):
    scaled = upstream * norm_gain
    mean_scaled = jnp.mean(scaled, axis=-1, keepdims=True)
    mean_proj = jnp.mean(scaled * normed, axis=-1, keepdims=True)
    return inv_std * (scaled - mean_scaled - normed * mean_proj)


def dot(left, right):
    return jnp.dot(left, right, preferred_element_type=F32)


def dot_rows(left, right):
    return lax.dot_general(left, right, (((0,), (0,)), ((), ())), preferred_element_type=F32)


def dot_cols(left, right):
    return lax.dot_general(left, right, (((1,), (1,)), ((), ())), preferred_element_type=F32)


def score_block(queries, keys_part, head_size):
    scores = jnp.einsum("sqhd,skhd->shqk", queries, keys_part, preferred_element_type=F32)
    return scores * head_size ** (-0.5)


def attend(queries, keys_part, values_part, alive):
    scores = score_block(queries, keys_part, queries.shape[-1])
    log_total = jnp.log(jnp.sum(jnp.exp(scores) * alive, axis=-1, keepdims=True))
    probs_half = (jnp.exp(scores - log_total) * alive).astype(BF16)
    context = jnp.einsum("shqk,skhd->sqhd", probs_half, values_part, preferred_element_type=F32)
    return context.astype(BF16), log_total


def attend_back(queries, keys_part, values_part, alive, log_total, grad_heads):
    head_size = queries.shape[-1]
    scores = score_block(queries, keys_part, head_size)
    probs_full = jnp.exp(scores - log_total) * alive
    probs_half = probs_full.astype(BF16)
    grad_values = jnp.einsum("shqk,sqhd->skhd", probs_half, grad_heads, preferred_element_type=F32)
    grad_probs = jnp.einsum("sqhd,skhd->shqk", grad_heads, values_part, preferred_element_type=F32)
    grad_scores = probs_full * (
        grad_probs - jnp.sum(probs_full * grad_probs, axis=-1, keepdims=True)
    )
    grad_half = (grad_scores * head_size ** (-0.5)).astype(BF16)
    grad_queries = jnp.einsum("shqk,skhd->sqhd", grad_half, keys_part, preferred_element_type=F32)
    grad_keys = jnp.einsum("shqk,sqhd->skhd", grad_half, queries, preferred_element_type=F32)
    return grad_queries, grad_keys, grad_values


def build(num_rep, num_shard):
    parts = num_shard * CORES
    bits = []
    step = CORES
    while step < num_rep:
        bits.append(step)
        step *= 2

    def flip(value, bit):
        return lax.ppermute(value, "rep", [(i, i ^ bit) for i in range(num_rep)])

    def sibling(value):
        return flip(value, 1)

    def turn(value, by):
        pairs = [(i, (i + by) % num_shard) for i in range(num_shard)]
        return lax.ppermute(value, "shard", pairs)

    def in_order(relative, shard_at):
        placed = []
        for place in range(num_shard):
            behind = (shard_at - place) % num_shard
            item = relative[0]
            for k in range(1, num_shard):
                item = jnp.where(behind == k, relative[k], item)
            placed.append(item)
        return placed

    def on_device(
        tokens, lengths, cotangent, qkv_weight, query_bias, value_bias, out_weight, out_bias,
        norm1_gain, norm1_bias, up_weight, up_bias, down_weight, down_bias, norm2_gain, norm2_bias,
    ):
        rows, width = tokens.shape
        num_seqs = lengths.shape[0]
        span = rows // num_seqs
        depth = qkv_weight.shape[0]
        hidden_size = up_weight.shape[1]
        heads_here = HEADS // parts
        head_size = width // HEADS
        att_block = heads_here * head_size
        ff_block = hidden_size // parts
        rep_at = lax.axis_index("rep")
        shard_at = lax.axis_index("shard")
        core_at = rep_at % CORES
        offsets = range(1, num_shard)

        def gather_rows(own):
            near = [own, sibling(own)]
            far = []
            for k in offsets:
                came = turn(own, k)
                far.append([came, sibling(came)])
            return near, far

        def stack(near, far):
            return jnp.concatenate(near + [item for pair in far for item in pair], axis=0)

        def scatter_rows(partial):
            blocks = [partial[i * rows : (i + 1) * rows] for i in range(parts)]
            total = None
            for k in offsets:
                mine, other = blocks[2 * k], blocks[2 * k + 1]
                came = turn((mine + sibling(other)).astype(BF16), -k)
                total = came.astype(F32) if total is None else total + came.astype(F32)
            near = blocks[0] + sibling(blocks[1])
            return near if total is None else near + total

        qkv_cols = qkv_weight.reshape(depth, 3, num_shard, CORES, att_block)
        up_cols = up_weight.reshape(depth, num_shard, CORES, ff_block)

        def qkv_for(shard):
            piece = lax.dynamic_slice(
                qkv_cols, (0, 0, shard, core_at, 0), (depth, 3, 1, 1, att_block)
            )
            return piece.reshape(depth, 3 * att_block)

        def up_for(shard):
            start = (shard * CORES + core_at) * ff_block
            return lax.dynamic_slice(up_weight, (0, start), (depth, ff_block))

        small = jnp.stack(
            [out_bias, norm1_gain, norm1_bias, down_bias, norm2_gain, norm2_bias]
            + [jnp.pad(lengths.astype(BF16), (0, depth - num_seqs))]
        )
        small_rel = [small] + [turn(small, k) for k in offsets]
        qkv_rel = [qkv_for(shard_at)] + [turn(qkv_for((shard_at + k) % num_shard), k) for k in offsets]
        tok_near, tok_far = gather_rows(tokens)
        up_send = [up_for((shard_at + k) % num_shard) for k in offsets]
        up_send, qkv_rel = lax.optimization_barrier((up_send, qkv_rel))
        up_rel = [up_for(shard_at)] + [turn(item, k) for item, k in zip(up_send, offsets)]

        small_full = jnp.concatenate(in_order(small_rel, shard_at), axis=1).astype(F32)
        out_bias_full, gain1, shift1, down_bias_full, gain2, shift2 = (
            small_full[i] for i in range(6)
        )
        lens_near = small[6, :num_seqs]
        lens_all = [lens_near, sibling(small[6])[:num_seqs]]
        for k in offsets:
            lens_all += [small_rel[k][6, :num_seqs], sibling(small_rel[k][6])[:num_seqs]]
        lens_all = jnp.concatenate(lens_all).astype(F32)
        alive = (jnp.arange(span).astype(F32)[None, :] < lens_all[:, None]).astype(F32)
        alive = alive[:, None, None, :]

        qkv_mine = jnp.concatenate(in_order(qkv_rel, shard_at), axis=0)
        query_mine = lax.dynamic_slice(query_bias, (core_at * att_block,), (att_block,))
        value_mine = lax.dynamic_slice(value_bias, (core_at * att_block,), (att_block,))
        qkv_bias = jnp.concatenate([query_mine, jnp.zeros_like(query_mine), value_mine]).astype(F32)
        out_mine = lax.dynamic_slice(out_weight, (core_at * att_block, 0), (att_block, width))
        down_mine = lax.dynamic_slice(down_weight, (core_at * ff_block, 0), (ff_block, width))
        up_bias_mine = lax.dynamic_slice(up_bias, (core_at * ff_block,), (ff_block,)).astype(F32)

        tok_all = stack(tok_near, tok_far)
        all_rows = tok_all.shape[0]
        qkv_rows = (dot(tok_all, qkv_mine) + qkv_bias).astype(BF16)
        shaped = qkv_rows.reshape(all_rows // span, span, 3, heads_here, head_size)
        queries, keys_part, values_part = shaped[:, :, 0], shaped[:, :, 1], shaped[:, :, 2]
        context, log_total = attend(queries, keys_part, values_part, alive)
        context = context.reshape(all_rows, att_block)
        resid1 = tokens.astype(F32) + scatter_rows(dot(context, out_mine)) + out_bias_full
        hidden1, normed1, inv_std1 = norm_rows(resid1, gain1, shift1)
        hid_all = stack(*gather_rows(hidden1.astype(BF16)))

        up_mine = jnp.concatenate(in_order(up_rel, shard_at), axis=0)
        pre_act = dot(hid_all, up_mine) + up_bias_mine
        activ = erf_gelu(pre_act).astype(BF16)
        resid2 = hidden1 + scatter_rows(dot(activ, down_mine)) + down_bias_full
        layer_f32, normed2, inv_std2 = norm_rows(resid2, gain2, shift2)
        layer_out = layer_f32.astype(BF16)

        upstream = cotangent.astype(F32)
        grad_gain2 = jnp.sum(upstream * normed2, axis=0)
        grad_shift2 = jnp.sum(upstream, axis=0)
        grad_resid2 = norm_back(upstream, normed2, inv_std2, gain2)
        grad_down_bias = jnp.sum(grad_resid2, axis=0)
        mlp_all = stack(*gather_rows(grad_resid2.astype(BF16)))
        sum_down = dot_rows(activ, mlp_all).astype(BF16)
        grad_pre = dot_cols(mlp_all, down_mine) * gelu_slope(pre_act)
        grad_pre_half = grad_pre.astype(BF16)
        grad_up_bias = jnp.sum(grad_pre, axis=0)
        sum_up = dot_rows(hid_all, grad_pre_half).astype(BF16)
        grad_hidden1 = grad_resid2 + scatter_rows(dot_cols(grad_pre_half, up_mine))
        grad_gain1 = jnp.sum(grad_hidden1 * normed1, axis=0)
        grad_shift1 = jnp.sum(grad_hidden1, axis=0)
        grad_resid1 = norm_back(grad_hidden1, normed1, inv_std1, gain1)
        grad_out_bias = jnp.sum(grad_resid1, axis=0)
        attn_all = stack(*gather_rows(grad_resid1.astype(BF16)))
        sum_out = dot_rows(context, attn_all).astype(BF16)
        grad_context = dot_cols(attn_all, out_mine).astype(BF16)
        grad_heads = grad_context.reshape(queries.shape)
        grad_queries, grad_keys, grad_values = attend_back(
            queries, keys_part, values_part, alive, log_total, grad_heads
        )
        grad_query_bias = jnp.sum(grad_queries, axis=(0, 1)).reshape(-1)
        grad_value_bias = jnp.sum(grad_values, axis=(0, 1)).reshape(-1)
        grad_qkv = jnp.concatenate(
            [g.reshape(all_rows, att_block) for g in (grad_queries, grad_keys, grad_values)], axis=1
        ).astype(BF16)
        sum_qkv = dot_rows(tok_all, grad_qkv).astype(BF16)
        input_grad = (grad_resid1 + scatter_rows(dot_cols(grad_qkv, qkv_mine))).astype(BF16)

        def bit_of(bit):
            return (rep_at // bit) % 2

        def halve(value, order, axis):
            for bit in order:
                side = bit_of(bit)
                half = value.shape[axis] // 2
                keep = lax.dynamic_slice_in_dim(value, side * half, half, axis)
                send = lax.dynamic_slice_in_dim(value, (1 - side) * half, half, axis)
                came = flip(send, bit)
                value = (keep.astype(F32) + came.astype(F32)).astype(BF16)
            return value

        def double(value, order, axis):
            for bit in reversed(order):
                came = flip(value, bit)
                low = bit_of(bit) == 0
                value = jnp.concatenate(
                    [jnp.where(low, value, came), jnp.where(low, came, value)], axis=axis
                )
            return value

        def both_cores(value):
            other = sibling(value)
            first = core_at == 0
            return jnp.where(first, value, other), jnp.where(first, other, value)

        def reduce_by_rows(value, order):
            value = double(halve(value, order, 0), order, 0)
            return jnp.concatenate(both_cores(value), axis=0).astype(F32)

        def reduce_by_columns(value, order):
            piece = halve(value, order, 1)
            relative = [lax.dynamic_index_in_dim(piece, shard_at, 0, keepdims=False)]
            for k in offsets:
                out_to = lax.dynamic_index_in_dim(piece, (shard_at + k) % num_shard, 0, keepdims=False)
                relative.append(turn(out_to, k))
            placed = jnp.stack(in_order(relative, shard_at), axis=1)
            full = double(placed, order, 0)
            return jnp.stack(both_cores(full), axis=2).astype(F32)

        late = bits[1:] + bits[:1]
        total_down = reduce_by_rows(sum_down, bits)
        total_up = reduce_by_columns(sum_up.reshape(num_shard, depth, ff_block), late)
        total_out = reduce_by_rows(sum_out, bits)
        total_qkv = reduce_by_columns(sum_qkv.reshape(num_shard, depth, 3 * att_block), bits)
        total_up = total_up.reshape(depth, hidden_size)
        total_qkv = total_qkv.reshape(depth, num_shard, CORES, 3, att_block)
        total_qkv = total_qkv.transpose(0, 3, 1, 2, 4).reshape(depth, 3 * width)

        row_sums = jnp.stack(
            [grad_out_bias, grad_gain1, grad_shift1, grad_down_bias, grad_gain2, grad_shift2]
        )
        row_sums = row_sums.reshape(6, num_shard, depth)
        mine = lax.dynamic_index_in_dim(row_sums, shard_at, 1, keepdims=False)
        for k in offsets:
            there = lax.dynamic_index_in_dim(row_sums, (shard_at + k) % num_shard, 1, keepdims=False)
            mine = mine + turn(there, k)
        mine = mine + sibling(mine)
        block_sums = jnp.concatenate([grad_query_bias, grad_value_bias, grad_up_bias])
        packed = jnp.concatenate([mine.reshape(-1), block_sums])
        for bit in bits:
            packed = packed + flip(packed, bit)
        mine = packed[: 6 * depth].reshape(6, depth)
        block_sums = packed[6 * depth :]
        first, second = both_cores(block_sums)
        total_query = jnp.concatenate([first[:att_block], second[:att_block]])
        total_value = jnp.concatenate(
            [first[att_block : 2 * att_block], second[att_block : 2 * att_block]]
        )
        total_up_bias = jnp.concatenate([first[2 * att_block :], second[2 * att_block :]])
        return (
            layer_out, input_grad, total_qkv, total_query, total_value, total_out,
            mine[0], mine[1], mine[2], total_up, total_up_bias, total_down, mine[3], mine[4], mine[5],
        )

    return on_device


def solution(mesh):
    rows, group, flat = P(("rep", "shard"), None), P("shard", None), P("shard")
    in_specs = (
        rows, P(("rep", "shard")), rows, group, flat, flat, group, flat, flat, flat,
        group, flat, group, flat, flat, flat,
    )
    out_specs = (
        rows, rows, group, flat, flat, group, flat, flat, flat, group, flat, group, flat, flat, flat,
    )
    return jax.shard_map(
        build(mesh.shape["rep"], mesh.shape["shard"]),
        mesh=mesh, in_specs=in_specs, out_specs=out_specs, check_vma=False,
    )
```

```python
import jax
import jax.numpy as jnp
from jax import lax
from jax.experimental import pallas as pl
from jax.experimental.pallas import tpu as pltpu
from jax.sharding import PartitionSpec as P

HEADS = 16
CORES = 2

EPS = 1e-06
ROOT_HALF = 0.7071067811865476
INV_ROOT_TAU = 0.3989422804014327

F32 = jnp.float32
BF16 = jnp.bfloat16


def erf_gelu(inputs):
    return 0.5 * inputs * (1.0 + jax.scipy.special.erf(inputs * ROOT_HALF))


def gelu_slope(inputs):
    cumul = 0.5 * (1.0 + jax.scipy.special.erf(inputs * ROOT_HALF))
    return cumul + inputs * jnp.exp(-0.5 * inputs * inputs) * INV_ROOT_TAU


def norm_rows(rows_in, norm_gain, norm_shift):
    row_mean = jnp.mean(rows_in, axis=-1, keepdims=True)
    centred = rows_in - row_mean
    variance = jnp.mean(centred * centred, axis=-1, keepdims=True)
    inv_std = lax.rsqrt(variance + EPS)
    normed = centred * inv_std
    return (normed * norm_gain + norm_shift, normed, inv_std)


def norm_back(upstream, normed, inv_std, norm_gain):
    scaled = upstream * norm_gain
    mean_scaled = jnp.mean(scaled, axis=-1, keepdims=True)
    mean_proj = jnp.mean(scaled * normed, axis=-1, keepdims=True)
    return inv_std * (scaled - mean_scaled - normed * mean_proj)


def dot(left, right):
    return jnp.dot(left, right, preferred_element_type=F32)


def dot_rows(left, right):
    return lax.dot_general(left, right, (((0,), (0,)), ((), ())), preferred_element_type=F32)


def dot_cols(left, right):
    return lax.dot_general(left, right, (((1,), (1,)), ((), ())), preferred_element_type=F32)


def alive_rows(small_refs, i, s, span, along):
    length = small_refs[i][6:7, s : s + 1].astype(F32)
    return lax.broadcasted_iota(jnp.int32, (span, span), along).astype(F32) < length


def attend_kernel(plan, at_ref, *refs):
    blocks, pieces, seqs, heads, size = plan
    toks, refs = refs[:blocks], refs[blocks:]
    smalls, refs = refs[:blocks], refs[blocks:]
    weights, refs = refs[:pieces], refs[pieces:]
    bias_ref, out_ref, tok_ref, qkv_ref, context_ref = refs[:5]
    partials = refs[5:]
    rows = toks[0].shape[0]
    depth = weights[0].shape[0]
    span = rows // seqs
    block = heads * size
    for i in range(blocks):
        tok_ref[i * rows : (i + 1) * rows, :] = toks[i][...]
    acc = jnp.broadcast_to(bias_ref[...], (blocks * rows, 3 * block))
    for k in range(pieces):
        columns = pl.ds(pl.multiple_of(at_ref[k] * depth, depth), depth)
        acc = acc + dot(tok_ref[:, columns], weights[k][...])
    qkv_ref[...] = acc.astype(BF16)
    for i in range(blocks):
        for s in range(seqs):
            alive = alive_rows(smalls, i, s, span, 1)
            first = i * rows + s * span
            here = qkv_ref[first : first + span, :]
            outs = []
            for h in range(heads):
                queries = here[:, h * size : (h + 1) * size]
                keys = here[:, block + h * size : block + (h + 1) * size]
                values = here[:, 2 * block + h * size : 2 * block + (h + 1) * size]
                weight = jnp.where(alive, jnp.exp(dot_cols(queries, keys) * size ** (-0.5)), 0.0)
                probs = weight * (1.0 / jnp.sum(weight, axis=-1, keepdims=True))
                outs.append(dot(probs.astype(BF16), values))
            context_ref[first : first + span, :] = jnp.concatenate(outs, axis=1).astype(BF16)
    result = dot(context_ref[...], out_ref[...])
    for i in range(blocks):
        partials[i][...] = result[i * rows : (i + 1) * rows]


def attend_back_kernel(plan, *refs):
    blocks, _, seqs, heads, size = plan
    grads, refs = refs[:blocks], refs[blocks:]
    smalls, refs = refs[:blocks], refs[blocks:]
    qkv_ref, out_ref, all_ref, grad_ref, sums_ref, back_ref = refs
    rows = grads[0].shape[0]
    span = rows // seqs
    block = heads * size
    for i in range(blocks):
        all_ref[i * rows : (i + 1) * rows, :] = grads[i][...]
    back_ref[...] = dot_cols(all_ref[...], out_ref[...]).astype(BF16)
    query_sum = jnp.zeros((1, block), F32)
    value_sum = jnp.zeros((1, block), F32)
    for i in range(blocks):
        for s in range(seqs):
            alive = alive_rows(smalls, i, s, span, 0)
            first = i * rows + s * span
            here = qkv_ref[first : first + span, :]
            grad_here = back_ref[first : first + span, :]
            by_query, by_key, by_value = [], [], []
            for h in range(heads):
                queries = here[:, h * size : (h + 1) * size]
                keys = here[:, block + h * size : block + (h + 1) * size]
                values = here[:, 2 * block + h * size : 2 * block + (h + 1) * size]
                grad = grad_here[:, h * size : (h + 1) * size]
                weight = jnp.where(alive, jnp.exp(dot_cols(keys, queries) * size ** (-0.5)), 0.0)
                probs = weight * (1.0 / jnp.sum(weight, axis=0, keepdims=True))
                by_value.append(dot(probs.astype(BF16), grad))
                grad_probs = dot_cols(values, grad)
                mean = jnp.sum(probs * grad_probs, axis=0, keepdims=True)
                grad_half = (probs * (grad_probs - mean) * size ** (-0.5)).astype(BF16)
                by_query.append(dot_rows(grad_half, keys))
                by_key.append(dot(grad_half, queries))
            by_query = jnp.concatenate(by_query, axis=1)
            by_key = jnp.concatenate(by_key, axis=1)
            by_value = jnp.concatenate(by_value, axis=1)
            query_sum = query_sum + jnp.sum(by_query, axis=0, keepdims=True)
            value_sum = value_sum + jnp.sum(by_value, axis=0, keepdims=True)
            grad_ref[first : first + span, :] = jnp.concatenate(
                [by_query, by_key, by_value], axis=1
            ).astype(BF16)
    sums_ref[...] = jnp.concatenate([query_sum, value_sum], axis=0)


def whole(count):
    return [pl.BlockSpec(memory_space=pltpu.VMEM)] * count


SCALARS = pl.BlockSpec(memory_space=pltpu.SMEM)
ROOMY = pltpu.CompilerParams(vmem_limit_bytes=48 * 1024 * 1024)


def take_columns(weight, index, block, repeats):
    depth, width = weight.shape
    each = width // repeats
    if block % 128:
        return jnp.concatenate(
            [
                lax.dynamic_slice(weight, (0, t * each + index * block), (depth, block))
                for t in range(repeats)
            ],
            axis=1,
        )

    def kernel(at_ref, in_ref, out_ref, sems):
        copies = []
        for t in range(repeats):
            start = pl.multiple_of(t * each + at_ref[0] * block, 128)
            copies.append(
                pltpu.make_async_copy(
                    in_ref.at[:, pl.ds(start, block)],
                    out_ref.at[:, t * block : (t + 1) * block],
                    sems.at[t],
                )
            )
        for copy in copies:
            copy.start()
        for copy in copies:
            copy.wait()

    return pl.pallas_call(
        kernel,
        in_specs=[SCALARS, pl.BlockSpec(memory_space=pl.ANY)],
        out_specs=whole(1)[0],
        out_shape=jax.ShapeDtypeStruct((depth, repeats * block), weight.dtype),
        scratch_shapes=[pltpu.SemaphoreType.DMA((repeats,))],
        name="take_columns",
    )(index.reshape(1).astype(jnp.int32), weight)


def merge_rows(mine, other, core_at):
    block, width = mine.shape
    tall = min(block, 256)
    steps = block // tall

    def kernel(at_ref, mine_ref, other_ref, out_ref):
        @pl.when(pl.program_id(0) == at_ref[0])
        def _():
            out_ref[...] = mine_ref[...].astype(F32)

        @pl.when(pl.program_id(0) != at_ref[0])
        def _():
            out_ref[...] = other_ref[...].astype(F32)

    return pl.pallas_call(
        kernel,
        grid_spec=pltpu.PrefetchScalarGridSpec(
            num_scalar_prefetch=1,
            grid=(CORES, steps),
            in_specs=[
                pl.BlockSpec((tall, width), lambda h, i, at: (jnp.where(h == at[0], i, 0), 0)),
                pl.BlockSpec((tall, width), lambda h, i, at: (jnp.where(h == at[0], 0, i), 0)),
            ],
            out_specs=pl.BlockSpec((tall, width), lambda h, i, at: (h * steps + i, 0)),
        ),
        out_shape=jax.ShapeDtypeStruct((CORES * block, width), F32),
        name="merge_rows",
    )(core_at.reshape(1).astype(jnp.int32), mine, other)


def merge_columns(mine, other, core_at, num_shard, repeats):
    rows, width = mine.shape
    each = width // (num_shard * repeats)
    if each % 128:
        pair = [jnp.where(core_at == 0, mine, other), jnp.where(core_at == 0, other, mine)]
        pair = jnp.stack([p.reshape(rows, num_shard, repeats, each) for p in pair], axis=3)
        return pair.transpose(0, 2, 1, 3, 4).reshape(rows, CORES * width).astype(F32)
    tall = min(rows, 64)

    def kernel(at_ref, mine_ref, other_ref, out_ref):
        def write(pair):
            for t in range(repeats):
                for p in range(num_shard):
                    for c in range(CORES):
                        to = ((t * num_shard + p) * CORES + c) * each
                        frm = (p * repeats + t) * each
                        out_ref[:, to : to + each] = pair[c][:, frm : frm + each].astype(F32)

        @pl.when(at_ref[0] == 0)
        def _():
            write((mine_ref, other_ref))

        @pl.when(at_ref[0] != 0)
        def _():
            write((other_ref, mine_ref))

    return pl.pallas_call(
        kernel,
        grid_spec=pltpu.PrefetchScalarGridSpec(
            num_scalar_prefetch=1,
            grid=(rows // tall,),
            in_specs=[pl.BlockSpec((tall, width), lambda i, at: (i, 0))] * 2,
            out_specs=pl.BlockSpec((tall, CORES * width), lambda i, at: (i, 0)),
        ),
        out_shape=jax.ShapeDtypeStruct((rows, CORES * width), F32),
        name="merge_columns",
    )(core_at.reshape(1).astype(jnp.int32), mine, other)


def build(num_rep, num_shard):
    parts = num_shard * CORES
    bits = []
    step = CORES
    while step < num_rep:
        bits.append(step)
        step *= 2

    orders = (bits, bits[1::-1] + bits[2:])

    def flip(value, bit):
        return lax.ppermute(value, "rep", [(i, i ^ bit) for i in range(num_rep)])

    def step_flip(value, stage):
        return lax.ppermute(
            value, "rep", [(i, i ^ orders[i % CORES][stage]) for i in range(num_rep)]
        )

    def sibling(value):
        return flip(value, 1)

    def turn(value, by):
        pairs = [(i, (i + by) % num_shard) for i in range(num_shard)]
        return lax.ppermute(value, "shard", pairs)

    def in_order(relative, shard_at):
        placed = []
        for place in range(num_shard):
            behind = (shard_at - place) % num_shard
            item = relative[0]
            for k in range(1, num_shard):
                item = jnp.where(behind == k, relative[k], item)
            placed.append(item)
        return placed

    def on_device(
        tokens, lengths, cotangent, qkv_weight, query_bias, value_bias, out_weight, out_bias,
        norm1_gain, norm1_bias, up_weight, up_bias, down_weight, down_bias, norm2_gain, norm2_bias,
    ):
        rows, width = tokens.shape
        num_seqs = lengths.shape[0]
        depth = qkv_weight.shape[0]
        hidden_size = up_weight.shape[1]
        heads_here = HEADS // parts
        head_size = width // HEADS
        att_block = heads_here * head_size
        ff_block = hidden_size // parts
        rep_at = lax.axis_index("rep")
        shard_at = lax.axis_index("shard")
        core_at = rep_at % CORES
        offsets = range(1, num_shard)

        def gather_rows(own):
            far = []
            for k in offsets:
                far.append(turn(own, k))
            near = [own, sibling(own)]
            far = [[came, sibling(came)] for came in far]
            return near, far

        def stack(near, far):
            return jnp.concatenate(near + [item for pair in far for item in pair], axis=0)

        def split(partial):
            return [partial[i * rows : (i + 1) * rows] for i in range(parts)]

        def scatter_rows(blocks):
            total = None
            for k in offsets:
                other = sibling(blocks[2 * k + 1])
                came = turn((blocks[2 * k] + other).astype(BF16), -k).astype(F32)
                total = came if total is None else total + came
            near = blocks[0] + sibling(blocks[1])
            return near if total is None else near + total

        def qkv_for(shard):
            return take_columns(qkv_weight, shard * CORES + core_at, att_block, 3)

        def up_for(shard):
            return take_columns(up_weight, shard * CORES + core_at, ff_block, 1)

        qkv_send = [qkv_for((shard_at + k) % num_shard) for k in offsets]
        qkv_rel = [turn(item, k) for item, k in zip(qkv_send, offsets)]
        tok_near, tok_far = gather_rows(tokens)
        small = jnp.concatenate(
            [out_bias, norm1_gain, norm1_bias, down_bias, norm2_gain, norm2_bias]
            + [jnp.pad(lengths.astype(BF16), (0, depth - num_seqs))]
        ).reshape(7, depth)
        small_near, small_far = gather_rows(small)
        small_rel = [small] + [pair[0] for pair in small_far]
        qkv_rel = [qkv_for(shard_at)] + qkv_rel
        up_send = [up_for((shard_at + k) % num_shard) for k in offsets]
        up_own = up_for(shard_at)
        up_send, qkv_rel = lax.optimization_barrier((up_send, qkv_rel))
        up_side = (rep_at // bits[0]) % 2
        up_rel = [up_own]
        for item, k in zip(up_send, offsets):
            half = lax.dynamic_slice_in_dim(item, up_side * (depth // 2), depth // 2, 0)
            half = turn(half, k)
            other = flip(half, bits[0])
            low = up_side == 0
            up_rel.append(
                jnp.concatenate([jnp.where(low, half, other), jnp.where(low, other, half)], axis=0)
            )

        small_full = jnp.concatenate(in_order(small_rel, shard_at), axis=1).astype(F32)
        out_bias_full, gain1, shift1, down_bias_full, gain2, shift2 = (
            small_full[i] for i in range(6)
        )
        came_from = (shard_at - jnp.arange(num_shard, dtype=jnp.int32)) % num_shard
        small_all = small_near + [item for pair in small_far for item in pair]

        qkv_mine = jnp.concatenate(in_order(qkv_rel, shard_at), axis=0)
        query_mine = lax.dynamic_slice(query_bias, (core_at * att_block,), (att_block,))
        value_mine = lax.dynamic_slice(value_bias, (core_at * att_block,), (att_block,))
        qkv_bias = jnp.concatenate([query_mine, jnp.zeros_like(query_mine), value_mine]).astype(F32)
        out_mine = lax.dynamic_slice(out_weight, (core_at * att_block, 0), (att_block, width))
        down_mine = lax.dynamic_slice(down_weight, (core_at * ff_block, 0), (ff_block, width))
        up_bias_mine = lax.dynamic_slice(up_bias, (core_at * ff_block,), (ff_block,)).astype(F32)

        all_rows = parts * rows
        plan = (parts, num_shard, num_seqs, heads_here, head_size)
        tok_all, qkv_rows, context, *partials = pl.pallas_call(
            lambda *refs: attend_kernel(plan, *refs),
            in_specs=[SCALARS] + whole(2 * parts + num_shard + 2),
            out_specs=whole(3 + parts),
            out_shape=[
                jax.ShapeDtypeStruct((all_rows, width), BF16),
                jax.ShapeDtypeStruct((all_rows, 3 * att_block), BF16),
                jax.ShapeDtypeStruct((all_rows, att_block), BF16),
            ]
            + [jax.ShapeDtypeStruct((rows, width), F32)] * parts,
            compiler_params=ROOMY,
            name="attend",
        )(
            came_from, *tok_near, *[item for pair in tok_far for item in pair], *small_all,
            *qkv_rel, qkv_bias.reshape(1, -1), out_mine,
        )
        resid1 = tokens.astype(F32) + scatter_rows(partials) + out_bias_full
        hidden1, normed1, inv_std1 = norm_rows(resid1, gain1, shift1)
        hidden1_half, up_rel = lax.optimization_barrier((hidden1.astype(BF16), up_rel))
        hid_all = stack(*gather_rows(hidden1_half))

        up_mine = jnp.concatenate(in_order(up_rel, shard_at), axis=0)
        pre_act = dot(hid_all, up_mine) + up_bias_mine
        activ = erf_gelu(pre_act).astype(BF16)
        resid2 = hidden1 + scatter_rows(split(dot(activ, down_mine))) + down_bias_full
        layer_f32, normed2, inv_std2 = norm_rows(resid2, gain2, shift2)
        layer_out = layer_f32.astype(BF16)

        upstream = cotangent.astype(F32)
        grad_gain2 = jnp.sum(upstream * normed2, axis=0)
        grad_shift2 = jnp.sum(upstream, axis=0)
        grad_resid2 = norm_back(upstream, normed2, inv_std2, gain2)
        grad_down_bias = jnp.sum(grad_resid2, axis=0)
        mlp_all = stack(*gather_rows(grad_resid2.astype(BF16)))
        sum_down = dot_rows(activ, mlp_all).astype(BF16)
        grad_pre = dot_cols(mlp_all, down_mine) * gelu_slope(pre_act)
        grad_pre_half = grad_pre.astype(BF16)
        grad_up_bias = jnp.sum(grad_pre, axis=0)
        sum_up = dot_rows(hid_all, grad_pre_half).astype(BF16)
        grad_hidden1 = grad_resid2 + scatter_rows(split(dot_cols(grad_pre_half, up_mine)))
        grad_gain1 = jnp.sum(grad_hidden1 * normed1, axis=0)
        grad_shift1 = jnp.sum(grad_hidden1, axis=0)
        grad_resid1 = norm_back(grad_hidden1, normed1, inv_std1, gain1)
        grad_out_bias = jnp.sum(grad_resid1, axis=0)
        attn_near, attn_far = gather_rows(grad_resid1.astype(BF16))
        attn_all, grad_qkv, bias_sums = pl.pallas_call(
            lambda *refs: attend_back_kernel(plan, *refs),
            in_specs=whole(2 * parts + 2),
            out_specs=whole(3),
            out_shape=[
                jax.ShapeDtypeStruct((all_rows, width), BF16),
                jax.ShapeDtypeStruct((all_rows, 3 * att_block), BF16),
                jax.ShapeDtypeStruct((2, att_block), F32),
            ],
            scratch_shapes=[pltpu.VMEM((all_rows, att_block), BF16)],
            compiler_params=ROOMY,
            name="attend_back",
        )(
            *attn_near, *[item for pair in attn_far for item in pair], *small_all,
            qkv_rows, out_mine,
        )
        sum_out = dot_rows(context, attn_all).astype(BF16)
        grad_query_bias, grad_value_bias = bias_sums[0], bias_sums[1]
        sum_qkv = dot_rows(tok_all, grad_qkv).astype(BF16)
        input_grad = (grad_resid1 + scatter_rows(split(dot_cols(grad_qkv, qkv_mine)))).astype(BF16)

        def side_at(stage):
            bit = jnp.where(core_at == 0, orders[0][stage], orders[1][stage])
            return (rep_at // bit) % 2

        def halve(value, axis):
            for stage in range(len(bits)):
                side = side_at(stage)
                half = value.shape[axis] // 2
                keep = lax.dynamic_slice_in_dim(value, side * half, half, axis)
                send = lax.dynamic_slice_in_dim(value, (1 - side) * half, half, axis)
                came = step_flip(send, stage)
                value = (keep.astype(F32) + came.astype(F32)).astype(BF16)
            return value

        def double(value):
            for stage in reversed(range(len(bits))):
                came = step_flip(value, stage)
                low = side_at(stage) == 0
                value = jnp.concatenate(
                    [jnp.where(low, value, came), jnp.where(low, came, value)], axis=0
                )
            return value

        def both_cores(value):
            other = sibling(value)
            first = core_at == 0
            return jnp.where(first, value, other), jnp.where(first, other, value)

        def reduce_by_rows(value):
            value = double(halve(value, 0))
            other = sibling(value)
            return merge_rows(value, other, core_at)

        def reduce_by_columns(value, repeats):
            piece = halve(value.reshape(num_shard, depth, -1), 1)
            relative = [lax.dynamic_index_in_dim(piece, shard_at, 0, keepdims=False)]
            for k in offsets:
                out_to = lax.dynamic_index_in_dim(piece, (shard_at + k) % num_shard, 0, keepdims=False)
                relative.append(turn(out_to, k))
            full = double(jnp.concatenate(in_order(relative, shard_at), axis=1))
            other = sibling(full)
            return merge_columns(full, other, core_at, num_shard, repeats)

        total_down = reduce_by_rows(sum_down)
        total_up = reduce_by_columns(sum_up, 1)
        total_out = reduce_by_rows(sum_out)
        total_qkv = reduce_by_columns(sum_qkv, 3)

        row_sums = jnp.stack(
            [grad_out_bias, grad_gain1, grad_shift1, grad_down_bias, grad_gain2, grad_shift2]
        )
        row_sums = row_sums.reshape(6, num_shard, depth)
        mine = lax.dynamic_index_in_dim(row_sums, shard_at, 1, keepdims=False)
        for k in offsets:
            there = lax.dynamic_index_in_dim(row_sums, (shard_at + k) % num_shard, 1, keepdims=False)
            mine = mine + turn(there, k)
        mine = mine + sibling(mine)
        block_sums = jnp.concatenate([grad_query_bias, grad_value_bias, grad_up_bias])
        packed = jnp.concatenate([mine.reshape(-1), block_sums])
        for bit in bits:
            packed = packed + flip(packed, bit)
        mine = packed[: 6 * depth].reshape(6, depth)
        block_sums = packed[6 * depth :]
        first, second = both_cores(block_sums)
        total_query = jnp.concatenate([first[:att_block], second[:att_block]])
        total_value = jnp.concatenate(
            [first[att_block : 2 * att_block], second[att_block : 2 * att_block]]
        )
        total_up_bias = jnp.concatenate([first[2 * att_block :], second[2 * att_block :]])
        return (
            layer_out, input_grad, total_qkv, total_query, total_value, total_out,
            mine[0], mine[1], mine[2], total_up, total_up_bias, total_down, mine[3], mine[4], mine[5],
        )

    return on_device


def solution(mesh):
    rows, group, flat = P(("rep", "shard"), None), P("shard", None), P("shard")
    in_specs = (
        rows, P(("rep", "shard")), rows, group, flat, flat, group, flat, flat, flat,
        group, flat, group, flat, flat, flat,
    )
    out_specs = (
        rows, rows, group, flat, flat, group, flat, flat, flat, group, flat, group, flat, flat, flat,
    )
    return jax.shard_map(
        build(mesh.shape["rep"], mesh.shape["shard"]),
        mesh=mesh, in_specs=in_specs, out_specs=out_specs, check_vma=False,
    )
```

```python
import math

import jax
import jax.numpy as jnp
from jax import lax
from jax.experimental import pallas as pl
from jax.experimental.pallas import tpu as pltpu
from jax.sharding import PartitionSpec as P

HEADS = 16
CORES = 2

EPS = 1e-06
ROOT_HALF = 0.7071067811865476
INV_ROOT_TAU = 0.3989422804014327

F32 = jnp.float32
BF16 = jnp.bfloat16


def erf_gelu(inputs):
    return 0.5 * inputs * (1.0 + jax.scipy.special.erf(inputs * ROOT_HALF))


def gelu_slope(inputs):
    cumul = 0.5 * (1.0 + jax.scipy.special.erf(inputs * ROOT_HALF))
    return cumul + inputs * jnp.exp(-0.5 * inputs * inputs) * INV_ROOT_TAU


def norm_rows(rows_in, norm_gain, norm_shift):
    row_mean = jnp.mean(rows_in, axis=-1, keepdims=True)
    centred = rows_in - row_mean
    variance = jnp.mean(centred * centred, axis=-1, keepdims=True)
    inv_std = lax.rsqrt(variance + EPS)
    normed = centred * inv_std
    return (normed * norm_gain + norm_shift, normed, inv_std)


def norm_back(upstream, normed, inv_std, norm_gain):
    scaled = upstream * norm_gain
    mean_scaled = jnp.mean(scaled, axis=-1, keepdims=True)
    mean_proj = jnp.mean(scaled * normed, axis=-1, keepdims=True)
    return inv_std * (scaled - mean_scaled - normed * mean_proj)


def dot(left, right):
    return jnp.dot(left, right, preferred_element_type=F32)


def dot_rows(left, right):
    return lax.dot_general(left, right, (((0,), (0,)), ((), ())), preferred_element_type=F32)


def dot_cols(left, right):
    return lax.dot_general(left, right, (((1,), (1,)), ((), ())), preferred_element_type=F32)


def alive_rows(small_refs, i, s, span, along):
    length = small_refs[i][6:7, s : s + 1].astype(F32)
    return lax.broadcasted_iota(jnp.int32, (span, span), along).astype(F32) < length


def attend_kernel(plan, at_ref, *refs):
    blocks, pieces, seqs, heads, size = plan
    toks, refs = refs[:blocks], refs[blocks:]
    smalls, refs = refs[:blocks], refs[blocks:]
    weights, refs = refs[:pieces], refs[pieces:]
    bias_ref, out_ref, refs = refs[0], refs[1], refs[2:]
    late, partials, refs = refs[:4], refs[4 : 4 + blocks], refs[4 + blocks :]
    tok_ref, weight_ref, qkv_ref, context_ref, sems = refs
    copies = [
        pltpu.make_async_copy(frm, to, sems.at[n])
        for n, (frm, to) in enumerate(zip((tok_ref, weight_ref, qkv_ref, context_ref), late))
    ]
    rows = toks[0].shape[0]
    depth = weights[0].shape[0]
    span = rows // seqs
    block = heads * size
    for i in range(blocks):
        tok_ref[i * rows : (i + 1) * rows, :] = toks[i][...]
    copies[0].start()
    for k in range(pieces):
        weight_ref[pl.ds(pl.multiple_of(at_ref[k] * depth, depth), depth), :] = weights[k][...]
    copies[1].start()
    qkv_ref[...] = (dot(tok_ref[...], weight_ref[...]) + bias_ref[...]).astype(BF16)
    copies[2].start()
    for i in range(blocks):
        for s in range(seqs):
            alive = alive_rows(smalls, i, s, span, 1)
            first = i * rows + s * span
            here = qkv_ref[first : first + span, :]
            outs = []
            for h in range(heads):
                queries = here[:, h * size : (h + 1) * size]
                keys = here[:, block + h * size : block + (h + 1) * size]
                values = here[:, 2 * block + h * size : 2 * block + (h + 1) * size]
                weight = jnp.where(alive, jnp.exp(dot_cols(queries, keys) * size ** (-0.5)), 0.0)
                probs = weight * (1.0 / jnp.sum(weight, axis=-1, keepdims=True))
                outs.append(dot(probs.astype(BF16), values))
            context_ref[first : first + span, :] = jnp.concatenate(outs, axis=1).astype(BF16)
    copies[3].start()
    result = dot(context_ref[...], out_ref[...])
    for i in range(blocks):
        partials[i][...] = result[i * rows : (i + 1) * rows]
    for copy in copies:
        copy.wait()


def attend_back_kernel(plan, *refs):
    blocks, _, seqs, heads, size = plan
    grads, refs = refs[:blocks], refs[blocks:]
    smalls, refs = refs[:blocks], refs[blocks:]
    qkv_ref, out_ref, all_ref, grad_ref, sums_ref, back_ref = refs
    rows = grads[0].shape[0]
    span = rows // seqs
    block = heads * size
    for i in range(blocks):
        all_ref[i * rows : (i + 1) * rows, :] = grads[i][...]
    back_ref[...] = dot_cols(all_ref[...], out_ref[...]).astype(BF16)
    query_sum = jnp.zeros((1, block), F32)
    value_sum = jnp.zeros((1, block), F32)
    for i in range(blocks):
        for s in range(seqs):
            alive = alive_rows(smalls, i, s, span, 0)
            first = i * rows + s * span
            here = qkv_ref[first : first + span, :]
            grad_here = back_ref[first : first + span, :]
            by_query, by_key, by_value = [], [], []
            for h in range(heads):
                queries = here[:, h * size : (h + 1) * size]
                keys = here[:, block + h * size : block + (h + 1) * size]
                values = here[:, 2 * block + h * size : 2 * block + (h + 1) * size]
                grad = grad_here[:, h * size : (h + 1) * size]
                weight = jnp.where(alive, jnp.exp(dot_cols(keys, queries) * size ** (-0.5)), 0.0)
                probs = weight * (1.0 / jnp.sum(weight, axis=0, keepdims=True))
                by_value.append(dot(probs.astype(BF16), grad))
                grad_probs = dot_cols(values, grad)
                mean = jnp.sum(probs * grad_probs, axis=0, keepdims=True)
                grad_half = (probs * (grad_probs - mean) * size ** (-0.5)).astype(BF16)
                by_query.append(dot_rows(grad_half, keys))
                by_key.append(dot(grad_half, queries))
            by_query = jnp.concatenate(by_query, axis=1)
            by_key = jnp.concatenate(by_key, axis=1)
            by_value = jnp.concatenate(by_value, axis=1)
            query_sum = query_sum + jnp.sum(by_query, axis=0, keepdims=True)
            value_sum = value_sum + jnp.sum(by_value, axis=0, keepdims=True)
            grad_ref[first : first + span, :] = jnp.concatenate(
                [by_query, by_key, by_value], axis=1
            ).astype(BF16)
    sums_ref[...] = jnp.concatenate([query_sum, value_sum], axis=0)


def whole(count):
    return [pl.BlockSpec(memory_space=pltpu.VMEM)] * count


SCALARS = pl.BlockSpec(memory_space=pltpu.SMEM)
MEBI = 1024 * 1024


def vmem(*shapes, spare=2):
    used = sum(math.prod(item.shape) * item.dtype.itemsize for item in shapes)
    return pltpu.CompilerParams(vmem_limit_bytes=min(used + spare * MEBI, 60 * MEBI))


def take_columns(weight, index, block, repeats, grant=4):
    depth, width = weight.shape
    each = width // repeats
    if block % 128:
        return jnp.concatenate(
            [
                lax.dynamic_slice(weight, (0, t * each + index * block), (depth, block))
                for t in range(repeats)
            ],
            axis=1,
        )

    def kernel(at_ref, in_ref, out_ref, sems):
        copies = []
        for t in range(repeats):
            start = pl.multiple_of(t * each + at_ref[0] * block, 128)
            copies.append(
                pltpu.make_async_copy(
                    in_ref.at[:, pl.ds(start, block)],
                    out_ref.at[:, t * block : (t + 1) * block],
                    sems.at[t],
                )
            )
        for copy in copies:
            copy.start()
        for copy in copies:
            copy.wait()

    return pl.pallas_call(
        kernel,
        in_specs=[SCALARS, pl.BlockSpec(memory_space=pltpu.HBM)],
        out_specs=whole(1)[0],
        out_shape=jax.ShapeDtypeStruct((depth, repeats * block), weight.dtype),
        scratch_shapes=[pltpu.SemaphoreType.DMA((repeats,))],
        compiler_params=pltpu.CompilerParams(vmem_limit_bytes=grant * MEBI),
        name="take_columns",
    )(index.reshape(1).astype(jnp.int32), pltpu.with_memory_space_constraint(weight, pltpu.HBM))


def merge_rows(mine, other, core_at):
    block, width = mine.shape
    tall = min(block, 256)
    steps = block // tall

    def kernel(at_ref, mine_ref, other_ref, out_ref):
        @pl.when(pl.program_id(0) == at_ref[0])
        def _():
            out_ref[...] = mine_ref[...].astype(F32)

        @pl.when(pl.program_id(0) != at_ref[0])
        def _():
            out_ref[...] = other_ref[...].astype(F32)

    return pl.pallas_call(
        kernel,
        grid_spec=pltpu.PrefetchScalarGridSpec(
            num_scalar_prefetch=1,
            grid=(CORES, steps),
            in_specs=[
                pl.BlockSpec((tall, width), lambda h, i, at: (jnp.where(h == at[0], i, 0), 0)),
                pl.BlockSpec((tall, width), lambda h, i, at: (jnp.where(h == at[0], 0, i), 0)),
            ],
            out_specs=pl.BlockSpec((tall, width), lambda h, i, at: (h * steps + i, 0)),
        ),
        out_shape=jax.ShapeDtypeStruct((CORES * block, width), F32),
        compiler_params=pltpu.CompilerParams(vmem_limit_bytes=6 * MEBI),
        name="merge_rows",
    )(core_at.reshape(1).astype(jnp.int32), mine, other)


def swapped(step, steps, swap):
    per = steps // 4
    quarter = step // per
    inner = jnp.logical_and(swap, jnp.logical_and(quarter > 0, quarter < 3))
    return jnp.where(inner, 3 * per - quarter * per + step % per, step)


def merge_columns(mine, other, core_at, num_shard, repeats, swap):
    rows, width = mine.shape
    each = width // (num_shard * repeats)
    if each % 128:
        if swap:
            tall = rows // 4

            def straight(item):
                return jnp.concatenate([item[q * tall : (q + 1) * tall] for q in (0, 2, 1, 3)])

            mine = jnp.where(core_at == 1, straight(mine), mine)
            other = jnp.where(core_at == 0, straight(other), other)
        pair = [jnp.where(core_at == 0, mine, other), jnp.where(core_at == 0, other, mine)]
        pair = jnp.stack([p.reshape(rows, num_shard, repeats, each) for p in pair], axis=3)
        return pair.transpose(0, 2, 1, 3, 4).reshape(rows, CORES * width).astype(F32)
    tall = min(rows // 4, 64)
    steps = rows // tall

    def place(i, core):
        return swapped(i, steps, core == 1) if swap else i

    def kernel(at_ref, mine_ref, other_ref, out_ref):
        def write(pair):
            for t in range(repeats):
                for p in range(num_shard):
                    for c in range(CORES):
                        to = ((t * num_shard + p) * CORES + c) * each
                        frm = (p * repeats + t) * each
                        out_ref[:, to : to + each] = pair[c][:, frm : frm + each].astype(F32)

        @pl.when(at_ref[0] == 0)
        def _():
            write((mine_ref, other_ref))

        @pl.when(at_ref[0] != 0)
        def _():
            write((other_ref, mine_ref))

    return pl.pallas_call(
        kernel,
        grid_spec=pltpu.PrefetchScalarGridSpec(
            num_scalar_prefetch=1,
            grid=(rows // tall,),
            in_specs=[
                pl.BlockSpec((tall, width), lambda i, at: (place(i, at[0]), 0)),
                pl.BlockSpec((tall, width), lambda i, at: (place(i, 1 - at[0]), 0)),
            ],
            out_specs=pl.BlockSpec((tall, CORES * width), lambda i, at: (i, 0)),
        ),
        out_shape=jax.ShapeDtypeStruct((rows, CORES * width), F32),
        compiler_params=pltpu.CompilerParams(vmem_limit_bytes=6 * MEBI),
        name="merge_columns",
    )(core_at.reshape(1).astype(jnp.int32), mine, other)


def build(num_rep, num_shard):
    parts = num_shard * CORES
    bits = []
    step = CORES
    while step < num_rep:
        bits.append(step)
        step *= 2

    mixed = (bits, bits[1::-1] + bits[2:])
    plain = (bits, bits)
    routes = {"down": mixed, "up": mixed, "qkv": plain, "out": mixed}
    backs = {"down": mixed, "up": mixed, "qkv": mixed, "out": mixed}

    def flip(value, bit):
        return lax.ppermute(value, "rep", [(i, i ^ bit) for i in range(num_rep)])

    def step_flip(value, route, stage):
        return lax.ppermute(
            value, "rep", [(i, i ^ route[i % CORES][stage]) for i in range(num_rep)]
        )

    def sibling(value):
        return flip(value, 1)

    def turn(value, by):
        pairs = [(i, (i + by) % num_shard) for i in range(num_shard)]
        return lax.ppermute(value, "shard", pairs)

    def in_order(relative, shard_at):
        placed = []
        for place in range(num_shard):
            behind = (shard_at - place) % num_shard
            item = relative[0]
            for k in range(1, num_shard):
                item = jnp.where(behind == k, relative[k], item)
            placed.append(item)
        return placed

    def on_device(
        tokens, lengths, cotangent, qkv_weight, query_bias, value_bias, out_weight, out_bias,
        norm1_gain, norm1_bias, up_weight, up_bias, down_weight, down_bias, norm2_gain, norm2_bias,
    ):
        rows, width = tokens.shape
        num_seqs = lengths.shape[0]
        depth = qkv_weight.shape[0]
        hidden_size = up_weight.shape[1]
        heads_here = HEADS // parts
        head_size = width // HEADS
        att_block = heads_here * head_size
        ff_block = hidden_size // parts
        rep_at = lax.axis_index("rep")
        shard_at = lax.axis_index("shard")
        core_at = rep_at % CORES
        offsets = range(1, num_shard)

        def gather_rows(own):
            far = []
            for k in offsets:
                far.append(turn(own, k))
            near = [own, sibling(own)]
            far = [[came, sibling(came)] for came in far]
            return near, far

        def stack(near, far):
            return jnp.concatenate(near + [item for pair in far for item in pair], axis=0)

        def split(partial):
            return [partial[i * rows : (i + 1) * rows] for i in range(parts)]

        def scatter_rows(blocks):
            total = None
            for k in offsets:
                other = sibling(blocks[2 * k + 1])
                came = turn((blocks[2 * k] + other).astype(BF16), -k).astype(F32)
                total = came if total is None else total + came
            near = blocks[0] + sibling(blocks[1])
            return near if total is None else near + total

        def qkv_for(shard, grant=4):
            return take_columns(qkv_weight, shard * CORES + core_at, att_block, 3, grant)

        def up_for(shard):
            return take_columns(up_weight, shard * CORES + core_at, ff_block, 1)

        qkv_send = [qkv_for((shard_at + k) % num_shard, 60) for k in offsets]
        qkv_rel = [turn(item, k) for item, k in zip(qkv_send, offsets)]
        tok_near, tok_far = gather_rows(tokens)
        small = jnp.concatenate(
            [out_bias, norm1_gain, norm1_bias, down_bias, norm2_gain, norm2_bias]
            + [jnp.pad(lengths.astype(BF16), (0, depth - num_seqs))]
        ).reshape(7, depth)
        small_near, small_far = gather_rows(small)
        small_rel = [small] + [pair[0] for pair in small_far]
        qkv_rel = [qkv_for(shard_at)] + qkv_rel
        up_send = [up_for((shard_at + k) % num_shard) for k in offsets]
        up_own = up_for(shard_at)
        up_send, qkv_rel = lax.optimization_barrier((up_send, qkv_rel))
        up_side = (rep_at // bits[0]) % 2
        up_rel = [up_own]
        for item, k in zip(up_send, offsets):
            half = lax.dynamic_slice_in_dim(item, up_side * (depth // 2), depth // 2, 0)
            half = turn(half, k)
            other = flip(half, bits[0])
            low = up_side == 0
            up_rel.append(
                jnp.concatenate([jnp.where(low, half, other), jnp.where(low, other, half)], axis=0)
            )

        small_full = jnp.concatenate(in_order(small_rel, shard_at), axis=1).astype(F32)
        out_bias_full, gain1, shift1, down_bias_full, gain2, shift2 = (
            small_full[i] for i in range(6)
        )
        came_from = (shard_at - jnp.arange(num_shard, dtype=jnp.int32)) % num_shard
        small_all = small_near + [item for pair in small_far for item in pair]

        query_mine = lax.dynamic_slice(query_bias, (core_at * att_block,), (att_block,))
        value_mine = lax.dynamic_slice(value_bias, (core_at * att_block,), (att_block,))
        qkv_bias = jnp.concatenate([query_mine, jnp.zeros_like(query_mine), value_mine]).astype(F32)
        out_mine = lax.dynamic_slice(out_weight, (core_at * att_block, 0), (att_block, width))
        down_mine = lax.dynamic_slice(down_weight, (core_at * ff_block, 0), (ff_block, width))
        up_bias_mine = lax.dynamic_slice(up_bias, (core_at * ff_block,), (ff_block,)).astype(F32)

        all_rows = parts * rows
        plan = (parts, num_shard, num_seqs, heads_here, head_size)
        taken = [
            came_from, *tok_near, *[item for pair in tok_far for item in pair], *small_all,
            *qkv_rel, qkv_bias.reshape(1, -1), out_mine,
        ]
        given = [
            pltpu.HBM((all_rows, width), BF16),
            pltpu.HBM((width, 3 * att_block), BF16),
            pltpu.HBM((all_rows, 3 * att_block), BF16),
            pltpu.HBM((all_rows, att_block), BF16),
        ] + [jax.ShapeDtypeStruct((rows, width), F32)] * parts
        tok_all, qkv_mine, qkv_rows, context, *partials = pl.pallas_call(
            lambda *refs: attend_kernel(plan, *refs),
            in_specs=[SCALARS] + whole(2 * parts + num_shard + 2),
            out_specs=[pl.BlockSpec(memory_space=pltpu.HBM)] * 4 + whole(parts),
            out_shape=given,
            scratch_shapes=[pltpu.VMEM(item.shape, item.dtype) for item in given[:4]]
            + [pltpu.SemaphoreType.DMA((4,))],
            compiler_params=vmem(*taken, *given, spare=6),
            name="attend",
        )(*taken)
        resid1 = tokens.astype(F32) + scatter_rows(partials) + out_bias_full
        hidden1, normed1, inv_std1 = norm_rows(resid1, gain1, shift1)
        hid_all = stack(*gather_rows(hidden1.astype(BF16)))

        up_mine = jnp.concatenate(in_order(up_rel, shard_at), axis=0)
        pre_act = dot(hid_all, up_mine) + up_bias_mine
        activ = erf_gelu(pre_act).astype(BF16)
        slope = lax.optimization_barrier(gelu_slope(lax.optimization_barrier((pre_act, activ))[0]))
        resid2 = hidden1 + scatter_rows(split(dot(activ, down_mine))) + down_bias_full
        layer_f32, normed2, inv_std2 = norm_rows(resid2, gain2, shift2)
        layer_out = layer_f32.astype(BF16)

        upstream = cotangent.astype(F32)
        grad_gain2 = jnp.sum(upstream * normed2, axis=0)
        grad_shift2 = jnp.sum(upstream, axis=0)
        grad_resid2 = norm_back(upstream, normed2, inv_std2, gain2)
        grad_down_bias = jnp.sum(grad_resid2, axis=0)
        mlp_all = stack(*gather_rows(grad_resid2.astype(BF16)))
        sum_down = dot_rows(activ, mlp_all).astype(BF16)
        grad_pre = dot_cols(mlp_all, down_mine) * slope
        grad_pre_half = grad_pre.astype(BF16)
        grad_up_bias = jnp.sum(grad_pre, axis=0)
        sum_up = dot_rows(hid_all, grad_pre_half).astype(BF16)
        grad_hidden1 = grad_resid2 + scatter_rows(split(dot_cols(grad_pre_half, up_mine)))
        grad_gain1 = jnp.sum(grad_hidden1 * normed1, axis=0)
        grad_shift1 = jnp.sum(grad_hidden1, axis=0)
        grad_resid1 = norm_back(grad_hidden1, normed1, inv_std1, gain1)
        grad_out_bias = jnp.sum(grad_resid1, axis=0)
        attn_near, attn_far = gather_rows(grad_resid1.astype(BF16))
        taken = [
            *attn_near, *[item for pair in attn_far for item in pair], *small_all,
            qkv_rows, out_mine,
        ]
        given = [
            jax.ShapeDtypeStruct((all_rows, width), BF16),
            jax.ShapeDtypeStruct((all_rows, 3 * att_block), BF16),
            jax.ShapeDtypeStruct((2, att_block), F32),
        ]
        attn_all, grad_qkv, bias_sums = pl.pallas_call(
            lambda *refs: attend_back_kernel(plan, *refs),
            in_specs=whole(2 * parts + 2),
            out_specs=whole(3),
            out_shape=given,
            scratch_shapes=[pltpu.VMEM((all_rows, att_block), BF16)],
            compiler_params=vmem(*taken, *given, context, spare=6),
            name="attend_back",
        )(*taken)
        sum_out = dot_rows(context, attn_all).astype(BF16)
        grad_query_bias, grad_value_bias = bias_sums[0], bias_sums[1]
        sum_qkv = dot_rows(tok_all, grad_qkv).astype(BF16)
        input_sum = scatter_rows(split(dot_cols(grad_qkv, qkv_mine)))
        input_grad = (grad_resid1 + input_sum).astype(BF16)

        def side_at(route, stage):
            bit = jnp.where(core_at == 0, route[0][stage], route[1][stage])
            return (rep_at // bit) % 2

        def halve(value, axis, name):
            route = routes[name]
            for stage in range(len(bits)):
                side = side_at(route, stage)
                half = value.shape[axis] // 2
                send = lax.dynamic_slice_in_dim(value, (1 - side) * half, half, axis)
                came = step_flip(send, route, stage)
                keep = lax.dynamic_slice_in_dim(value, side * half, half, axis)
                value = (keep.astype(F32) + came.astype(F32)).astype(BF16)
            return value

        def double(value, name):
            route = backs[name]
            for stage in reversed(range(len(bits))):
                came = step_flip(value, route, stage)
                low = side_at(route, stage) == 0
                value = jnp.concatenate(
                    [jnp.where(low, value, came), jnp.where(low, came, value)], axis=0
                )
            return value

        def reduce_by_rows(value, name):
            value = double(halve(value, 0, name), name)
            other = sibling(value)
            return value, other

        def reduce_by_columns(value, repeats, name):
            piece = halve(value.reshape(num_shard, depth, -1), 1, name)
            relative = [lax.dynamic_index_in_dim(piece, shard_at, 0, keepdims=False)]
            for k in offsets:
                out_to = lax.dynamic_index_in_dim(piece, (shard_at + k) % num_shard, 0, keepdims=False)
                relative.append(turn(out_to, k))
            full = double(jnp.concatenate(in_order(relative, shard_at), axis=1), name)
            other = sibling(full)
            swap = routes[name] != backs[name]
            return merge_columns(full, other, core_at, num_shard, repeats, swap)

        total_down = merge_rows(*reduce_by_rows(sum_down, "down"), core_at)
        total_up = reduce_by_columns(sum_up, 1, "up")
        total_qkv = reduce_by_columns(sum_qkv, 3, "qkv")

        row_sums = jnp.stack(
            [grad_out_bias, grad_gain1, grad_shift1, grad_down_bias, grad_gain2, grad_shift2]
        )
        row_sums = row_sums.reshape(6, num_shard, depth)
        mine = lax.dynamic_index_in_dim(row_sums, shard_at, 1, keepdims=False)
        for k in offsets:
            there = lax.dynamic_index_in_dim(row_sums, (shard_at + k) % num_shard, 1, keepdims=False)
            mine = mine + turn(there, k)
        mine = mine + sibling(mine)
        packed = jnp.concatenate(
            [mine.reshape(-1), grad_query_bias, grad_value_bias, grad_up_bias]
        )
        beside = -(-packed.size // (128 * att_block)) * 128
        packed_rows = jnp.pad(packed, (0, att_block * beside - packed.size)).astype(BF16)
        sum_out = jnp.concatenate([sum_out, packed_rows.reshape(att_block, beside)], axis=1)
        out_here, out_there = reduce_by_rows(sum_out, "out")
        total_out = merge_rows(out_here[:, :width], out_there[:, :width], core_at)
        packed = out_here[:, width:].reshape(-1).astype(F32)
        packed_there = out_there[:, width:].reshape(-1).astype(F32)
        mine = packed[: 6 * depth].reshape(6, depth)
        block_sums = packed[6 * depth : 6 * depth + 2 * att_block + ff_block]
        other_sums = packed_there[6 * depth : 6 * depth + 2 * att_block + ff_block]
        first = jnp.where(core_at == 0, block_sums, other_sums)
        second = jnp.where(core_at == 0, other_sums, block_sums)
        total_query = jnp.concatenate([first[:att_block], second[:att_block]])
        total_value = jnp.concatenate(
            [first[att_block : 2 * att_block], second[att_block : 2 * att_block]]
        )
        total_up_bias = jnp.concatenate([first[2 * att_block :], second[2 * att_block :]])
        return (
            layer_out, input_grad, total_qkv, total_query, total_value, total_out,
            mine[0], mine[1], mine[2], total_up, total_up_bias, total_down, mine[3], mine[4], mine[5],
        )

    return on_device


def solution(mesh):
    rows, group, flat = P(("rep", "shard"), None), P("shard", None), P("shard")
    in_specs = (
        rows, P(("rep", "shard")), rows, group, flat, flat, group, flat, flat, flat,
        group, flat, group, flat, flat, flat,
    )
    out_specs = (
        rows, rows, group, flat, flat, group, flat, flat, flat, group, flat, group, flat, flat, flat,
    )
    return jax.shard_map(
        build(mesh.shape["rep"], mesh.shape["shard"]),
        mesh=mesh, in_specs=in_specs, out_specs=out_specs, check_vma=False,
    )
```

```python
import math

import jax
import jax.numpy as jnp
from jax import lax
from jax.experimental import pallas as pl
from jax.experimental.pallas import tpu as pltpu
from jax.sharding import PartitionSpec as P

HEADS = 16
CORES = 2

EPS = 1e-06
ROOT_HALF = 0.7071067811865476
INV_ROOT_TAU = 0.3989422804014327

F32 = jnp.float32
BF16 = jnp.bfloat16


def erf_gelu(inputs):
    return 0.5 * inputs * (1.0 + jax.scipy.special.erf(inputs * ROOT_HALF))


def gelu_slope(inputs):
    cumul = 0.5 * (1.0 + jax.scipy.special.erf(inputs * ROOT_HALF))
    return cumul + inputs * jnp.exp(-0.5 * inputs * inputs) * INV_ROOT_TAU


def norm_rows(rows_in, norm_gain, norm_shift):
    row_mean = jnp.mean(rows_in, axis=-1, keepdims=True)
    centred = rows_in - row_mean
    variance = jnp.mean(centred * centred, axis=-1, keepdims=True)
    inv_std = lax.rsqrt(variance + EPS)
    normed = centred * inv_std
    return (normed * norm_gain + norm_shift, normed, inv_std)


def norm_back(upstream, normed, inv_std, norm_gain):
    scaled = upstream * norm_gain
    mean_scaled = jnp.mean(scaled, axis=-1, keepdims=True)
    mean_proj = jnp.mean(scaled * normed, axis=-1, keepdims=True)
    return inv_std * (scaled - mean_scaled - normed * mean_proj)


def dot(left, right):
    return jnp.dot(left, right, preferred_element_type=F32)


def dot_rows(left, right):
    return lax.dot_general(left, right, (((0,), (0,)), ((), ())), preferred_element_type=F32)


def dot_cols(left, right):
    return lax.dot_general(left, right, (((1,), (1,)), ((), ())), preferred_element_type=F32)


def alive_rows(small_refs, i, s, span, along):
    length = small_refs[i][6:7, s : s + 1].astype(F32)
    return lax.broadcasted_iota(jnp.int32, (span, span), along).astype(F32) < length


def attend_kernel(plan, at_ref, *refs):
    blocks, pieces, seqs, heads, size = plan
    toks, refs = refs[:blocks], refs[blocks:]
    smalls, refs = refs[:blocks], refs[blocks:]
    weights, refs = refs[:pieces], refs[pieces:]
    bias_ref, out_ref, refs = refs[0], refs[1], refs[2:]
    late, partials, refs = refs[:4], refs[4 : 4 + blocks], refs[4 + blocks :]
    tok_ref, weight_ref, qkv_ref, context_ref, sems = refs
    copies = [
        pltpu.make_async_copy(frm, to, sems.at[n])
        for n, (frm, to) in enumerate(zip((tok_ref, weight_ref, qkv_ref, context_ref), late))
    ]
    rows = toks[0].shape[0]
    depth = weights[0].shape[0]
    span = rows // seqs
    block = heads * size
    for i in range(blocks):
        tok_ref[i * rows : (i + 1) * rows, :] = toks[i][...]
    copies[0].start()
    for k in range(pieces):
        weight_ref[pl.ds(pl.multiple_of(at_ref[k] * depth, depth), depth), :] = weights[k][...]
    copies[1].start()
    qkv_ref[...] = (dot(tok_ref[...], weight_ref[...]) + bias_ref[...]).astype(BF16)
    copies[2].start()
    for i in range(blocks):
        for s in range(seqs):
            alive = alive_rows(smalls, i, s, span, 1)
            first = i * rows + s * span
            here = qkv_ref[first : first + span, :]
            outs = []
            for h in range(heads):
                queries = here[:, h * size : (h + 1) * size]
                keys = here[:, block + h * size : block + (h + 1) * size]
                values = here[:, 2 * block + h * size : 2 * block + (h + 1) * size]
                weight = jnp.where(alive, jnp.exp(dot_cols(queries, keys) * size ** (-0.5)), 0.0)
                probs = weight * (1.0 / jnp.sum(weight, axis=-1, keepdims=True))
                outs.append(dot(probs.astype(BF16), values))
            context_ref[first : first + span, :] = jnp.concatenate(outs, axis=1).astype(BF16)
    copies[3].start()
    result = dot(context_ref[...], out_ref[...]).astype(BF16)
    for i in range(blocks):
        partials[i][...] = result[i * rows : (i + 1) * rows]
    for copy in copies:
        copy.wait()


def attend_back_kernel(plan, *refs):
    blocks, _, seqs, heads, size = plan
    grads, refs = refs[:blocks], refs[blocks:]
    smalls, refs = refs[:blocks], refs[blocks:]
    qkv_ref, out_ref, all_ref, grad_ref, sums_ref, back_ref = refs
    rows = grads[0].shape[0]
    span = rows // seqs
    block = heads * size
    for i in range(blocks):
        all_ref[i * rows : (i + 1) * rows, :] = grads[i][...]
    back_ref[...] = dot_cols(all_ref[...], out_ref[...]).astype(BF16)
    query_sum = jnp.zeros((1, block), F32)
    value_sum = jnp.zeros((1, block), F32)
    for i in range(blocks):
        for s in range(seqs):
            alive = alive_rows(smalls, i, s, span, 0)
            first = i * rows + s * span
            here = qkv_ref[first : first + span, :]
            grad_here = back_ref[first : first + span, :]
            by_query, by_key, by_value = [], [], []
            for h in range(heads):
                queries = here[:, h * size : (h + 1) * size]
                keys = here[:, block + h * size : block + (h + 1) * size]
                values = here[:, 2 * block + h * size : 2 * block + (h + 1) * size]
                grad = grad_here[:, h * size : (h + 1) * size]
                weight = jnp.where(alive, jnp.exp(dot_cols(keys, queries) * size ** (-0.5)), 0.0)
                probs = weight * (1.0 / jnp.sum(weight, axis=0, keepdims=True))
                by_value.append(dot(probs.astype(BF16), grad))
                grad_probs = dot_cols(values, grad)
                mean = jnp.sum(probs * grad_probs, axis=0, keepdims=True)
                grad_half = (probs * (grad_probs - mean) * size ** (-0.5)).astype(BF16)
                by_query.append(dot_rows(grad_half, keys))
                by_key.append(dot(grad_half, queries))
            by_query = jnp.concatenate(by_query, axis=1)
            by_key = jnp.concatenate(by_key, axis=1)
            by_value = jnp.concatenate(by_value, axis=1)
            query_sum = query_sum + jnp.sum(by_query, axis=0, keepdims=True)
            value_sum = value_sum + jnp.sum(by_value, axis=0, keepdims=True)
            grad_ref[first : first + span, :] = jnp.concatenate(
                [by_query, by_key, by_value], axis=1
            ).astype(BF16)
    sums_ref[...] = jnp.concatenate([query_sum, value_sum], axis=0)


def whole(count):
    return [pl.BlockSpec(memory_space=pltpu.VMEM)] * count


SCALARS = pl.BlockSpec(memory_space=pltpu.SMEM)
MEBI = 1024 * 1024


def vmem(*shapes, spare=2):
    used = sum(math.prod(item.shape) * item.dtype.itemsize for item in shapes)
    return pltpu.CompilerParams(vmem_limit_bytes=min(used + spare * MEBI, 60 * MEBI))


def take_columns(weight, index, block, repeats, grant=4, late=False):
    depth, width = weight.shape
    each = width // repeats
    if block % 128:
        return jnp.concatenate(
            [
                lax.dynamic_slice(weight, (0, t * each + index * block), (depth, block))
                for t in range(repeats)
            ],
            axis=1,
        )

    def kernel(at_ref, in_ref, out_ref, *scratch):
        held, sems = (scratch[0] if late else out_ref), scratch[-1]
        copies = []
        for t in range(repeats):
            start = pl.multiple_of(t * each + at_ref[0] * block, 128)
            copies.append(
                pltpu.make_async_copy(
                    in_ref.at[:, pl.ds(start, block)],
                    held.at[:, t * block : (t + 1) * block],
                    sems.at[t],
                )
            )
        for copy in copies:
            copy.start()
        for copy in copies:
            copy.wait()
        if late:
            copy = pltpu.make_async_copy(held, out_ref, sems.at[repeats])
            copy.start()
            copy.wait()

    shape = (depth, repeats * block)
    scratch_shapes = [pltpu.VMEM(shape, weight.dtype)] if late else []
    return pl.pallas_call(
        kernel,
        in_specs=[SCALARS, pl.BlockSpec(memory_space=pltpu.HBM)],
        out_specs=pl.BlockSpec(memory_space=pltpu.HBM) if late else whole(1)[0],
        out_shape=pltpu.HBM(shape, weight.dtype) if late else jax.ShapeDtypeStruct(shape, weight.dtype),
        scratch_shapes=scratch_shapes + [pltpu.SemaphoreType.DMA((repeats + 1,))],
        compiler_params=pltpu.CompilerParams(vmem_limit_bytes=grant * MEBI),
        name="take_columns",
    )(index.reshape(1).astype(jnp.int32), pltpu.with_memory_space_constraint(weight, pltpu.HBM))


def take_rows(weight, index, block):
    width = weight.shape[1]
    tall = min(block, 256)
    steps = block // tall

    def kernel(at_ref, in_ref, out_ref):
        out_ref[...] = in_ref[...]

    return pl.pallas_call(
        kernel,
        grid_spec=pltpu.PrefetchScalarGridSpec(
            num_scalar_prefetch=1,
            grid=(steps,),
            in_specs=[pl.BlockSpec((tall, width), lambda i, at: (at[0] * steps + i, 0))],
            out_specs=pl.BlockSpec((tall, width), lambda i, at: (i, 0)),
        ),
        out_shape=pltpu.HBM((block, width), weight.dtype),
        compiler_params=pltpu.CompilerParams(vmem_limit_bytes=4 * MEBI),
        name="take_rows",
    )(index.reshape(1).astype(jnp.int32), pltpu.with_memory_space_constraint(weight, pltpu.HBM))


def merge_rows(mine, other, core_at):
    block, width = mine.shape
    tall = min(block, 256)
    steps = block // tall

    def kernel(at_ref, mine_ref, other_ref, out_ref):
        @pl.when(pl.program_id(0) == at_ref[0])
        def _():
            out_ref[...] = mine_ref[...].astype(F32)

        @pl.when(pl.program_id(0) != at_ref[0])
        def _():
            out_ref[...] = other_ref[...].astype(F32)

    return pl.pallas_call(
        kernel,
        grid_spec=pltpu.PrefetchScalarGridSpec(
            num_scalar_prefetch=1,
            grid=(CORES, steps),
            in_specs=[
                pl.BlockSpec((tall, width), lambda h, i, at: (jnp.where(h == at[0], i, 0), 0)),
                pl.BlockSpec((tall, width), lambda h, i, at: (jnp.where(h == at[0], 0, i), 0)),
            ],
            out_specs=pl.BlockSpec((tall, width), lambda h, i, at: (h * steps + i, 0)),
        ),
        out_shape=jax.ShapeDtypeStruct((CORES * block, width), F32),
        compiler_params=pltpu.CompilerParams(vmem_limit_bytes=6 * MEBI),
        name="merge_rows",
    )(core_at.reshape(1).astype(jnp.int32), mine, other)


def swapped(step, steps, swap):
    per = steps // 4
    quarter = step // per
    inner = jnp.logical_and(swap, jnp.logical_and(quarter > 0, quarter < 3))
    return jnp.where(inner, 3 * per - quarter * per + step % per, step)


def merge_columns(mine, other, core_at, num_shard, repeats, swap):
    rows, width = mine.shape
    each = width // (num_shard * repeats)
    if each % 128:
        if swap:
            tall = rows // 4

            def straight(item):
                return jnp.concatenate([item[q * tall : (q + 1) * tall] for q in (0, 2, 1, 3)])

            mine = jnp.where(core_at == 1, straight(mine), mine)
            other = jnp.where(core_at == 0, straight(other), other)
        pair = [jnp.where(core_at == 0, mine, other), jnp.where(core_at == 0, other, mine)]
        pair = jnp.stack([p.reshape(rows, num_shard, repeats, each) for p in pair], axis=3)
        return pair.transpose(0, 2, 1, 3, 4).reshape(rows, CORES * width).astype(F32)
    tall = min(rows // 4, 64)
    steps = rows // tall

    def place(i, core):
        return swapped(i, steps, core == 1) if swap else i

    def kernel(at_ref, mine_ref, other_ref, out_ref):
        def write(pair):
            for t in range(repeats):
                for p in range(num_shard):
                    for c in range(CORES):
                        to = ((t * num_shard + p) * CORES + c) * each
                        frm = (p * repeats + t) * each
                        out_ref[:, to : to + each] = pair[c][:, frm : frm + each].astype(F32)

        @pl.when(at_ref[0] == 0)
        def _():
            write((mine_ref, other_ref))

        @pl.when(at_ref[0] != 0)
        def _():
            write((other_ref, mine_ref))

    return pl.pallas_call(
        kernel,
        grid_spec=pltpu.PrefetchScalarGridSpec(
            num_scalar_prefetch=1,
            grid=(rows // tall,),
            in_specs=[
                pl.BlockSpec((tall, width), lambda i, at: (place(i, at[0]), 0)),
                pl.BlockSpec((tall, width), lambda i, at: (place(i, 1 - at[0]), 0)),
            ],
            out_specs=pl.BlockSpec((tall, CORES * width), lambda i, at: (i, 0)),
        ),
        out_shape=jax.ShapeDtypeStruct((rows, CORES * width), F32),
        compiler_params=pltpu.CompilerParams(vmem_limit_bytes=6 * MEBI),
        name="merge_columns",
    )(core_at.reshape(1).astype(jnp.int32), mine, other)


def build(num_rep, num_shard):
    parts = num_shard * CORES
    bits = []
    step = CORES
    while step < num_rep:
        bits.append(step)
        step *= 2

    mixed = (bits, bits[1::-1] + bits[2:])
    plain = (bits, bits)
    routes = {"down": mixed, "up": mixed, "qkv": plain, "out": mixed}
    backs = {"down": mixed, "up": mixed, "qkv": mixed, "out": mixed}

    def flip(value, bit):
        return lax.ppermute(value, "rep", [(i, i ^ bit) for i in range(num_rep)])

    def step_flip(value, route, stage):
        return lax.ppermute(
            value, "rep", [(i, i ^ route[i % CORES][stage]) for i in range(num_rep)]
        )

    def sibling(value):
        return flip(value, 1)

    def turn(value, by):
        pairs = [(i, (i + by) % num_shard) for i in range(num_shard)]
        return lax.ppermute(value, "shard", pairs)

    def in_order(relative, shard_at):
        placed = []
        for place in range(num_shard):
            behind = (shard_at - place) % num_shard
            item = relative[0]
            for k in range(1, num_shard):
                item = jnp.where(behind == k, relative[k], item)
            placed.append(item)
        return placed

    def on_device(
        tokens, lengths, cotangent, qkv_weight, query_bias, value_bias, out_weight, out_bias,
        norm1_gain, norm1_bias, up_weight, up_bias, down_weight, down_bias, norm2_gain, norm2_bias,
    ):
        rows, width = tokens.shape
        num_seqs = lengths.shape[0]
        depth = qkv_weight.shape[0]
        hidden_size = up_weight.shape[1]
        heads_here = HEADS // parts
        head_size = width // HEADS
        att_block = heads_here * head_size
        ff_block = hidden_size // parts
        rep_at = lax.axis_index("rep")
        shard_at = lax.axis_index("shard")
        core_at = rep_at % CORES
        offsets = range(1, num_shard)

        def gather_rows(own):
            far = []
            for k in offsets:
                far.append(turn(own, k))
            near = [own, sibling(own)]
            far = [[came, sibling(came)] for came in far]
            return near, far

        def stack(near, far):
            return jnp.concatenate(near + [item for pair in far for item in pair], axis=0)

        def split(partial):
            return [partial[i * rows : (i + 1) * rows] for i in range(parts)]

        def scatter_rows(blocks):
            total = None
            for k in offsets:
                other = sibling(blocks[2 * k + 1])
                both = blocks[2 * k].astype(F32) + other.astype(F32)
                came = turn(both.astype(BF16), -k).astype(F32)
                total = came if total is None else total + came
            near = blocks[0].astype(F32) + sibling(blocks[1]).astype(F32)
            return near if total is None else near + total

        def qkv_for(shard, grant=4):
            return take_columns(qkv_weight, shard * CORES + core_at, att_block, 3, grant)

        def up_for(shard):
            return take_columns(up_weight, shard * CORES + core_at, ff_block, 1, late=True)

        qkv_send = [qkv_for((shard_at + k) % num_shard, 60) for k in offsets]
        qkv_rel = [turn(item, k) for item, k in zip(qkv_send, offsets)]
        tok_near, tok_far = gather_rows(tokens)
        small = jnp.concatenate(
            [out_bias, norm1_gain, norm1_bias, down_bias, norm2_gain, norm2_bias]
            + [jnp.pad(lengths.astype(BF16), (0, depth - num_seqs))]
        ).reshape(7, depth)
        small_near, small_far = gather_rows(small)
        small_rel = [small] + [pair[0] for pair in small_far]
        qkv_rel = [qkv_for(shard_at)] + qkv_rel
        up_send = [up_for((shard_at + k) % num_shard) for k in offsets]
        up_own = up_for(shard_at)
        up_send, qkv_rel = lax.optimization_barrier((up_send, qkv_rel))
        up_side = (rep_at // bits[0]) % 2
        up_rel = [up_own]
        for item, k in zip(up_send, offsets):
            half = lax.dynamic_slice_in_dim(item, up_side * (depth // 2), depth // 2, 0)
            half = turn(half, k)
            other = flip(half, bits[0])
            low = up_side == 0
            up_rel.append(
                jnp.concatenate([jnp.where(low, half, other), jnp.where(low, other, half)], axis=0)
            )

        small_full = jnp.concatenate(in_order(small_rel, shard_at), axis=1).astype(F32)
        out_bias_full, gain1, shift1, down_bias_full, gain2, shift2 = (
            small_full[i] for i in range(6)
        )
        came_from = (shard_at - jnp.arange(num_shard, dtype=jnp.int32)) % num_shard
        small_all = small_near + [item for pair in small_far for item in pair]

        query_mine = lax.dynamic_slice(query_bias, (core_at * att_block,), (att_block,))
        value_mine = lax.dynamic_slice(value_bias, (core_at * att_block,), (att_block,))
        qkv_bias = jnp.concatenate([query_mine, jnp.zeros_like(query_mine), value_mine]).astype(F32)
        out_mine = lax.dynamic_slice(out_weight, (core_at * att_block, 0), (att_block, width))
        down_mine = take_rows(down_weight, core_at, ff_block)
        up_bias_mine = lax.dynamic_slice(up_bias, (core_at * ff_block,), (ff_block,)).astype(F32)

        all_rows = parts * rows
        plan = (parts, num_shard, num_seqs, heads_here, head_size)
        taken = [
            came_from, *tok_near, *[item for pair in tok_far for item in pair], *small_all,
            *qkv_rel, qkv_bias.reshape(1, -1), out_mine,
        ]
        given = [
            pltpu.HBM((all_rows, width), BF16),
            pltpu.HBM((width, 3 * att_block), BF16),
            pltpu.HBM((all_rows, 3 * att_block), BF16),
            pltpu.HBM((all_rows, att_block), BF16),
        ] + [jax.ShapeDtypeStruct((rows, width), BF16)] * parts
        tok_all, qkv_mine, qkv_rows, context, *partials = pl.pallas_call(
            lambda *refs: attend_kernel(plan, *refs),
            in_specs=[SCALARS] + whole(2 * parts + num_shard + 2),
            out_specs=[pl.BlockSpec(memory_space=pltpu.HBM)] * 4 + whole(parts),
            out_shape=given,
            scratch_shapes=[pltpu.VMEM(item.shape, item.dtype) for item in given[:4]]
            + [pltpu.SemaphoreType.DMA((4,))],
            compiler_params=vmem(*taken, *given, spare=6),
            name="attend",
        )(*taken)
        resid1 = tokens.astype(F32) + scatter_rows(partials) + out_bias_full
        hidden1, normed1, inv_std1 = norm_rows(resid1, gain1, shift1)
        hid_all = stack(*gather_rows(hidden1.astype(BF16)))

        up_mine = jnp.concatenate(in_order(up_rel, shard_at), axis=0)
        pre_act = dot(hid_all, up_mine) + up_bias_mine
        activ = erf_gelu(pre_act).astype(BF16)
        slope = lax.optimization_barrier(
            gelu_slope(lax.optimization_barrier((pre_act, activ))[0]).astype(BF16)
        )
        resid2 = hidden1 + scatter_rows(split(dot(activ, down_mine).astype(BF16))) + down_bias_full
        layer_f32, normed2, inv_std2 = norm_rows(resid2, gain2, shift2)
        layer_out = layer_f32.astype(BF16)

        upstream = cotangent.astype(F32)
        grad_gain2 = jnp.sum(upstream * normed2, axis=0)
        grad_shift2 = jnp.sum(upstream, axis=0)
        grad_resid2 = norm_back(upstream, normed2, inv_std2, gain2)
        grad_down_bias = jnp.sum(grad_resid2, axis=0)
        mlp_all = stack(*gather_rows(grad_resid2.astype(BF16)))
        sum_down = dot_rows(activ, mlp_all).astype(BF16)
        grad_pre = dot_cols(mlp_all, down_mine) * slope.astype(F32)
        grad_pre_half = grad_pre.astype(BF16)
        grad_up_bias = jnp.sum(grad_pre, axis=0)
        sum_up = dot_rows(hid_all, grad_pre_half).astype(BF16)
        grad_hidden1 = grad_resid2 + scatter_rows(split(dot_cols(grad_pre_half, up_mine).astype(BF16)))
        grad_gain1 = jnp.sum(grad_hidden1 * normed1, axis=0)
        grad_shift1 = jnp.sum(grad_hidden1, axis=0)
        grad_resid1 = norm_back(grad_hidden1, normed1, inv_std1, gain1)
        grad_out_bias = jnp.sum(grad_resid1, axis=0)
        attn_near, attn_far = gather_rows(grad_resid1.astype(BF16))
        taken = [
            *attn_near, *[item for pair in attn_far for item in pair], *small_all,
            qkv_rows, out_mine,
        ]
        given = [
            jax.ShapeDtypeStruct((all_rows, width), BF16),
            jax.ShapeDtypeStruct((all_rows, 3 * att_block), BF16),
            jax.ShapeDtypeStruct((2, att_block), F32),
        ]
        attn_all, grad_qkv, bias_sums = pl.pallas_call(
            lambda *refs: attend_back_kernel(plan, *refs),
            in_specs=whole(2 * parts + 2),
            out_specs=whole(3),
            out_shape=given,
            scratch_shapes=[pltpu.VMEM((all_rows, att_block), BF16)],
            compiler_params=vmem(*taken, *given, context, spare=6),
            name="attend_back",
        )(*taken)
        sum_out = dot_rows(context, attn_all).astype(BF16)
        grad_query_bias, grad_value_bias = bias_sums[0], bias_sums[1]
        sum_qkv = dot_rows(tok_all, grad_qkv).astype(BF16)
        input_sum = scatter_rows(split(dot_cols(grad_qkv, qkv_mine).astype(BF16)))
        input_grad = (grad_resid1 + input_sum).astype(BF16)

        def side_at(route, stage):
            bit = jnp.where(core_at == 0, route[0][stage], route[1][stage])
            return (rep_at // bit) % 2

        def halve(value, axis, name):
            route = routes[name]
            for stage in range(len(bits)):
                side = side_at(route, stage)
                half = value.shape[axis] // 2
                send = lax.dynamic_slice_in_dim(value, (1 - side) * half, half, axis)
                came = step_flip(send, route, stage)
                keep = lax.dynamic_slice_in_dim(value, side * half, half, axis)
                value = (keep.astype(F32) + came.astype(F32)).astype(BF16)
            return value

        def double(value, name):
            route = backs[name]
            for stage in reversed(range(len(bits))):
                came = step_flip(value, route, stage)
                low = side_at(route, stage) == 0
                value = jnp.concatenate(
                    [jnp.where(low, value, came), jnp.where(low, came, value)], axis=0
                )
            return value

        def reduce_by_rows(value, name):
            value = double(halve(value, 0, name), name)
            other = sibling(value)
            return value, other

        def reduce_by_columns(value, repeats, name):
            piece = halve(value.reshape(num_shard, depth, -1), 1, name)
            relative = [lax.dynamic_index_in_dim(piece, shard_at, 0, keepdims=False)]
            for k in offsets:
                out_to = lax.dynamic_index_in_dim(piece, (shard_at + k) % num_shard, 0, keepdims=False)
                relative.append(turn(out_to, k))
            full = double(jnp.concatenate(in_order(relative, shard_at), axis=1), name)
            other = sibling(full)
            swap = routes[name] != backs[name]
            return merge_columns(full, other, core_at, num_shard, repeats, swap)

        total_down = merge_rows(*reduce_by_rows(sum_down, "down"), core_at)
        total_up = reduce_by_columns(sum_up, 1, "up")
        total_qkv = reduce_by_columns(sum_qkv, 3, "qkv")

        row_sums = jnp.stack(
            [grad_out_bias, grad_gain1, grad_shift1, grad_down_bias, grad_gain2, grad_shift2]
        )
        row_sums = row_sums.reshape(6, num_shard, depth)
        mine = lax.dynamic_index_in_dim(row_sums, shard_at, 1, keepdims=False)
        for k in offsets:
            there = lax.dynamic_index_in_dim(row_sums, (shard_at + k) % num_shard, 1, keepdims=False)
            mine = mine + turn(there, k)
        mine = mine + sibling(mine)
        packed = jnp.concatenate(
            [mine.reshape(-1), grad_query_bias, grad_value_bias, grad_up_bias]
        )
        beside = -(-packed.size // (128 * att_block)) * 128
        packed_rows = jnp.pad(packed, (0, att_block * beside - packed.size)).astype(BF16)
        sum_out = jnp.concatenate([sum_out, packed_rows.reshape(att_block, beside)], axis=1)
        out_here, out_there = reduce_by_rows(sum_out, "out")
        total_out = merge_rows(out_here[:, :width], out_there[:, :width], core_at)
        packed = out_here[:, width:].reshape(-1).astype(F32)
        packed_there = out_there[:, width:].reshape(-1).astype(F32)
        mine = packed[: 6 * depth].reshape(6, depth)
        block_sums = packed[6 * depth : 6 * depth + 2 * att_block + ff_block]
        other_sums = packed_there[6 * depth : 6 * depth + 2 * att_block + ff_block]
        first = jnp.where(core_at == 0, block_sums, other_sums)
        second = jnp.where(core_at == 0, other_sums, block_sums)
        total_query = jnp.concatenate([first[:att_block], second[:att_block]])
        total_value = jnp.concatenate(
            [first[att_block : 2 * att_block], second[att_block : 2 * att_block]]
        )
        total_up_bias = jnp.concatenate([first[2 * att_block :], second[2 * att_block :]])
        return (
            layer_out, input_grad, total_qkv, total_query, total_value, total_out,
            mine[0], mine[1], mine[2], total_up, total_up_bias, total_down, mine[3], mine[4], mine[5],
        )

    return on_device


def solution(mesh):
    rows, group, flat = P(("rep", "shard"), None), P("shard", None), P("shard")
    in_specs = (
        rows, P(("rep", "shard")), rows, group, flat, flat, group, flat, flat, flat,
        group, flat, group, flat, flat, flat,
    )
    out_specs = (
        rows, rows, group, flat, flat, group, flat, flat, flat, group, flat, group, flat, flat, flat,
    )
    return jax.shard_map(
        build(mesh.shape["rep"], mesh.shape["shard"]),
        mesh=mesh, in_specs=in_specs, out_specs=out_specs, check_vma=False,
    )
```

```python
import math

import jax
import jax.numpy as jnp
from jax import lax
from jax.experimental import pallas as pl
from jax.experimental.pallas import tpu as pltpu
from jax.sharding import PartitionSpec as P

HEADS = 16
CORES = 2

EPS = 1e-06
ROOT_HALF = 0.7071067811865476
INV_ROOT_TAU = 0.3989422804014327

F32 = jnp.float32
BF16 = jnp.bfloat16


def erf_gelu(inputs):
    return 0.5 * inputs * (1.0 + jax.scipy.special.erf(inputs * ROOT_HALF))


def gelu_slope(inputs):
    cumul = 0.5 * (1.0 + jax.scipy.special.erf(inputs * ROOT_HALF))
    return cumul + inputs * jnp.exp(-0.5 * inputs * inputs) * INV_ROOT_TAU


def norm_rows(rows_in, norm_gain, norm_shift):
    row_mean = jnp.mean(rows_in, axis=-1, keepdims=True)
    centred = rows_in - row_mean
    variance = jnp.mean(centred * centred, axis=-1, keepdims=True)
    inv_std = lax.rsqrt(variance + EPS)
    normed = centred * inv_std
    return (normed * norm_gain + norm_shift, normed, inv_std)


def norm_back(upstream, normed, inv_std, norm_gain):
    scaled = upstream * norm_gain
    mean_scaled = jnp.mean(scaled, axis=-1, keepdims=True)
    mean_proj = jnp.mean(scaled * normed, axis=-1, keepdims=True)
    return inv_std * (scaled - mean_scaled - normed * mean_proj)


def dot(left, right):
    return jnp.dot(left, right, preferred_element_type=F32)


def dot_rows(left, right):
    return lax.dot_general(left, right, (((0,), (0,)), ((), ())), preferred_element_type=F32)


def dot_cols(left, right):
    return lax.dot_general(left, right, (((1,), (1,)), ((), ())), preferred_element_type=F32)


def alive_rows(small_refs, i, s, span, along):
    length = small_refs[i][6:7, s : s + 1].astype(F32)
    return lax.broadcasted_iota(jnp.int32, (span, span), along).astype(F32) < length


def attend_kernel(plan, at_ref, *refs):
    blocks, pieces, seqs, heads, size = plan
    toks, refs = refs[:blocks], refs[blocks:]
    smalls, refs = refs[:blocks], refs[blocks:]
    weights, refs = refs[:pieces], refs[pieces:]
    bias_ref, out_ref, refs = refs[0], refs[1], refs[2:]
    late, partials, refs = refs[:4], refs[4 : 4 + blocks], refs[4 + blocks :]
    tok_ref, weight_ref, qkv_ref, context_ref, sems = refs
    copies = [
        pltpu.make_async_copy(frm, to, sems.at[n])
        for n, (frm, to) in enumerate(zip((tok_ref, weight_ref, qkv_ref, context_ref), late))
    ]
    rows = toks[0].shape[0]
    depth = weights[0].shape[0]
    span = rows // seqs
    block = heads * size
    for i in range(blocks):
        tok_ref[i * rows : (i + 1) * rows, :] = toks[i][...]
    copies[0].start()
    for k in range(pieces):
        weight_ref[pl.ds(pl.multiple_of(at_ref[k] * depth, depth), depth), :] = weights[k][...]
    copies[1].start()
    qkv_ref[...] = (dot(tok_ref[...], weight_ref[...]) + bias_ref[...]).astype(BF16)
    copies[2].start()
    for i in range(blocks):
        for s in range(seqs):
            alive = alive_rows(smalls, i, s, span, 1)
            first = i * rows + s * span
            here = qkv_ref[first : first + span, :]
            outs = []
            for h in range(heads):
                queries = here[:, h * size : (h + 1) * size]
                keys = here[:, block + h * size : block + (h + 1) * size]
                values = here[:, 2 * block + h * size : 2 * block + (h + 1) * size]
                weight = jnp.where(alive, jnp.exp(dot_cols(queries, keys) * size ** (-0.5)), 0.0)
                probs = weight * (1.0 / jnp.sum(weight, axis=-1, keepdims=True))
                outs.append(dot(probs.astype(BF16), values))
            context_ref[first : first + span, :] = jnp.concatenate(outs, axis=1).astype(BF16)
    copies[3].start()
    result = dot(context_ref[...], out_ref[...]).astype(BF16)
    for i in range(blocks):
        partials[i][...] = result[i * rows : (i + 1) * rows]
    for copy in copies:
        copy.wait()


def attend_back_kernel(plan, *refs):
    blocks, _, seqs, heads, size = plan
    grads, refs = refs[:blocks], refs[blocks:]
    smalls, refs = refs[:blocks], refs[blocks:]
    qkv_ref, out_ref, all_ref, grad_ref, sums_ref, back_ref = refs
    rows = grads[0].shape[0]
    span = rows // seqs
    block = heads * size
    for i in range(blocks):
        all_ref[i * rows : (i + 1) * rows, :] = grads[i][...]
    back_ref[...] = dot_cols(all_ref[...], out_ref[...]).astype(BF16)
    query_sum = jnp.zeros((1, block), F32)
    value_sum = jnp.zeros((1, block), F32)
    for i in range(blocks):
        for s in range(seqs):
            alive = alive_rows(smalls, i, s, span, 0)
            first = i * rows + s * span
            here = qkv_ref[first : first + span, :]
            grad_here = back_ref[first : first + span, :]
            by_query, by_key, by_value = [], [], []
            for h in range(heads):
                queries = here[:, h * size : (h + 1) * size]
                keys = here[:, block + h * size : block + (h + 1) * size]
                values = here[:, 2 * block + h * size : 2 * block + (h + 1) * size]
                grad = grad_here[:, h * size : (h + 1) * size]
                weight = jnp.where(alive, jnp.exp(dot_cols(keys, queries) * size ** (-0.5)), 0.0)
                probs = weight * (1.0 / jnp.sum(weight, axis=0, keepdims=True))
                by_value.append(dot(probs.astype(BF16), grad))
                grad_probs = dot_cols(values, grad)
                mean = jnp.sum(probs * grad_probs, axis=0, keepdims=True)
                grad_half = (probs * (grad_probs - mean) * size ** (-0.5)).astype(BF16)
                by_query.append(dot_rows(grad_half, keys))
                by_key.append(dot(grad_half, queries))
            by_query = jnp.concatenate(by_query, axis=1)
            by_key = jnp.concatenate(by_key, axis=1)
            by_value = jnp.concatenate(by_value, axis=1)
            query_sum = query_sum + jnp.sum(by_query, axis=0, keepdims=True)
            value_sum = value_sum + jnp.sum(by_value, axis=0, keepdims=True)
            grad_ref[first : first + span, :] = jnp.concatenate(
                [by_query, by_key, by_value], axis=1
            ).astype(BF16)
    sums_ref[...] = jnp.concatenate([query_sum, value_sum], axis=0)


def whole(count):
    return [pl.BlockSpec(memory_space=pltpu.VMEM)] * count


SCALARS = pl.BlockSpec(memory_space=pltpu.SMEM)
MEBI = 1024 * 1024


def vmem(*shapes, spare=2):
    used = sum(math.prod(item.shape) * item.dtype.itemsize for item in shapes)
    return pltpu.CompilerParams(vmem_limit_bytes=min(used + spare * MEBI, 60 * MEBI))


def take_columns(weight, index, block, repeats, grant=4, late=False):
    depth, width = weight.shape
    each = width // repeats
    if block % 128:
        return jnp.concatenate(
            [
                lax.dynamic_slice(weight, (0, t * each + index * block), (depth, block))
                for t in range(repeats)
            ],
            axis=1,
        )

    def kernel(at_ref, in_ref, out_ref, *scratch):
        held, sems = (scratch[0] if late else out_ref), scratch[-1]
        copies = []
        for t in range(repeats):
            start = pl.multiple_of(t * each + at_ref[0] * block, 128)
            copies.append(
                pltpu.make_async_copy(
                    in_ref.at[:, pl.ds(start, block)],
                    held.at[:, t * block : (t + 1) * block],
                    sems.at[t],
                )
            )
        for copy in copies:
            copy.start()
        for copy in copies:
            copy.wait()
        if late:
            copy = pltpu.make_async_copy(held, out_ref, sems.at[repeats])
            copy.start()
            copy.wait()

    shape = (depth, repeats * block)
    scratch_shapes = [pltpu.VMEM(shape, weight.dtype)] if late else []
    return pl.pallas_call(
        kernel,
        in_specs=[SCALARS, pl.BlockSpec(memory_space=pltpu.HBM)],
        out_specs=pl.BlockSpec(memory_space=pltpu.HBM) if late else whole(1)[0],
        out_shape=pltpu.HBM(shape, weight.dtype) if late else jax.ShapeDtypeStruct(shape, weight.dtype),
        scratch_shapes=scratch_shapes + [pltpu.SemaphoreType.DMA((repeats + 1,))],
        compiler_params=pltpu.CompilerParams(vmem_limit_bytes=grant * MEBI),
        name="take_columns",
    )(index.reshape(1).astype(jnp.int32), pltpu.with_memory_space_constraint(weight, pltpu.HBM))


def take_rows(weight, index, block):
    width = weight.shape[1]
    tall = min(block, 256)
    steps = block // tall

    def kernel(at_ref, in_ref, out_ref):
        out_ref[...] = in_ref[...]

    return pl.pallas_call(
        kernel,
        grid_spec=pltpu.PrefetchScalarGridSpec(
            num_scalar_prefetch=1,
            grid=(steps,),
            in_specs=[pl.BlockSpec((tall, width), lambda i, at: (at[0] * steps + i, 0))],
            out_specs=pl.BlockSpec((tall, width), lambda i, at: (i, 0)),
        ),
        out_shape=pltpu.HBM((block, width), weight.dtype),
        compiler_params=pltpu.CompilerParams(vmem_limit_bytes=4 * MEBI),
        name="take_rows",
    )(index.reshape(1).astype(jnp.int32), pltpu.with_memory_space_constraint(weight, pltpu.HBM))


def merge_rows(mine, other, core_at):
    block, width = mine.shape
    tall = min(block, 256)
    steps = block // tall

    def kernel(at_ref, mine_ref, other_ref, out_ref):
        @pl.when(pl.program_id(0) == at_ref[0])
        def _():
            out_ref[...] = mine_ref[...].astype(F32)

        @pl.when(pl.program_id(0) != at_ref[0])
        def _():
            out_ref[...] = other_ref[...].astype(F32)

    return pl.pallas_call(
        kernel,
        grid_spec=pltpu.PrefetchScalarGridSpec(
            num_scalar_prefetch=1,
            grid=(CORES, steps),
            in_specs=[
                pl.BlockSpec((tall, width), lambda h, i, at: (jnp.where(h == at[0], i, 0), 0)),
                pl.BlockSpec((tall, width), lambda h, i, at: (jnp.where(h == at[0], 0, i), 0)),
            ],
            out_specs=pl.BlockSpec((tall, width), lambda h, i, at: (h * steps + i, 0)),
        ),
        out_shape=jax.ShapeDtypeStruct((CORES * block, width), F32),
        compiler_params=pltpu.CompilerParams(vmem_limit_bytes=6 * MEBI),
        name="merge_rows",
    )(core_at.reshape(1).astype(jnp.int32), mine, other)


def swapped(step, steps, swap):
    per = steps // 4
    quarter = step // per
    inner = jnp.logical_and(swap, jnp.logical_and(quarter > 0, quarter < 3))
    return jnp.where(inner, 3 * per - quarter * per + step % per, step)


def merge_columns(mine, other, core_at, num_shard, repeats, swap):
    rows, width = mine.shape
    each = width // (num_shard * repeats)
    if each % 128:
        if swap:
            tall = rows // 4

            def straight(item):
                return jnp.concatenate([item[q * tall : (q + 1) * tall] for q in (0, 2, 1, 3)])

            mine = jnp.where(core_at == 1, straight(mine), mine)
            other = jnp.where(core_at == 0, straight(other), other)
        pair = [jnp.where(core_at == 0, mine, other), jnp.where(core_at == 0, other, mine)]
        pair = jnp.stack([p.reshape(rows, num_shard, repeats, each) for p in pair], axis=3)
        return pair.transpose(0, 2, 1, 3, 4).reshape(rows, CORES * width).astype(F32)
    tall = min(rows // 4, 64)
    steps = rows // tall

    def place(i, core):
        return swapped(i, steps, core == 1) if swap else i

    def kernel(at_ref, mine_ref, other_ref, out_ref):
        def write(pair):
            for t in range(repeats):
                for p in range(num_shard):
                    for c in range(CORES):
                        to = ((t * num_shard + p) * CORES + c) * each
                        frm = (p * repeats + t) * each
                        out_ref[:, to : to + each] = pair[c][:, frm : frm + each].astype(F32)

        @pl.when(at_ref[0] == 0)
        def _():
            write((mine_ref, other_ref))

        @pl.when(at_ref[0] != 0)
        def _():
            write((other_ref, mine_ref))

    return pl.pallas_call(
        kernel,
        grid_spec=pltpu.PrefetchScalarGridSpec(
            num_scalar_prefetch=1,
            grid=(rows // tall,),
            in_specs=[
                pl.BlockSpec((tall, width), lambda i, at: (place(i, at[0]), 0)),
                pl.BlockSpec((tall, width), lambda i, at: (place(i, 1 - at[0]), 0)),
            ],
            out_specs=pl.BlockSpec((tall, CORES * width), lambda i, at: (i, 0)),
        ),
        out_shape=jax.ShapeDtypeStruct((rows, CORES * width), F32),
        compiler_params=pltpu.CompilerParams(vmem_limit_bytes=6 * MEBI),
        name="merge_columns",
    )(core_at.reshape(1).astype(jnp.int32), mine, other)


def build(num_rep, num_shard):
    parts = num_shard * CORES
    bits = []
    step = CORES
    while step < num_rep:
        bits.append(step)
        step *= 2

    mixed = (bits, bits[1::-1] + bits[2:])
    plain = (bits, bits)
    routes = {"down": mixed, "up": mixed, "qkv": plain, "out": mixed}
    backs = {"down": mixed, "up": mixed, "qkv": mixed, "out": mixed}

    def flip(value, bit):
        return lax.ppermute(value, "rep", [(i, i ^ bit) for i in range(num_rep)])

    def step_flip(value, route, stage):
        return lax.ppermute(
            value, "rep", [(i, i ^ route[i % CORES][stage]) for i in range(num_rep)]
        )

    def sibling(value):
        return flip(value, 1)

    def turn(value, by):
        pairs = [(i, (i + by) % num_shard) for i in range(num_shard)]
        return lax.ppermute(value, "shard", pairs)

    def in_order(relative, shard_at):
        placed = []
        for place in range(num_shard):
            behind = (shard_at - place) % num_shard
            item = relative[0]
            for k in range(1, num_shard):
                item = jnp.where(behind == k, relative[k], item)
            placed.append(item)
        return placed

    def on_device(
        tokens, lengths, cotangent, qkv_weight, query_bias, value_bias, out_weight, out_bias,
        norm1_gain, norm1_bias, up_weight, up_bias, down_weight, down_bias, norm2_gain, norm2_bias,
    ):
        rows, width = tokens.shape
        num_seqs = lengths.shape[0]
        depth = qkv_weight.shape[0]
        hidden_size = up_weight.shape[1]
        heads_here = HEADS // parts
        head_size = width // HEADS
        att_block = heads_here * head_size
        ff_block = hidden_size // parts
        rep_at = lax.axis_index("rep")
        shard_at = lax.axis_index("shard")
        core_at = rep_at % CORES
        offsets = range(1, num_shard)

        def gather_rows(own):
            far = []
            for k in offsets:
                far.append(turn(own, k))
            near = [own, sibling(own)]
            far = [[came, sibling(came)] for came in far]
            return near, far

        def stack(near, far):
            return jnp.concatenate(near + [item for pair in far for item in pair], axis=0)

        def split(partial):
            return [partial[i * rows : (i + 1) * rows] for i in range(parts)]

        def scatter_rows(blocks):
            total = None
            for k in offsets:
                other = sibling(blocks[2 * k + 1])
                both = blocks[2 * k].astype(F32) + other.astype(F32)
                came = turn(both.astype(BF16), -k).astype(F32)
                total = came if total is None else total + came
            near = blocks[0].astype(F32) + sibling(blocks[1]).astype(F32)
            return near if total is None else near + total

        def qkv_for(shard, grant=4):
            return take_columns(qkv_weight, shard * CORES + core_at, att_block, 3, grant)

        def up_for(shard):
            return take_columns(up_weight, shard * CORES + core_at, ff_block, 1, late=True)

        qkv_send = [qkv_for((shard_at + k) % num_shard, 60) for k in offsets]
        qkv_rel = [turn(item, k) for item, k in zip(qkv_send, offsets)]
        tok_near, tok_far = gather_rows(tokens)
        small = jnp.concatenate(
            [out_bias, norm1_gain, norm1_bias, down_bias, norm2_gain, norm2_bias]
            + [jnp.pad(lengths.astype(BF16), (0, depth - num_seqs))]
        ).reshape(7, depth)
        small_near, small_far = gather_rows(small)
        small_rel = [small] + [pair[0] for pair in small_far]
        qkv_rel = [qkv_for(shard_at)] + qkv_rel
        up_send = [up_for((shard_at + k) % num_shard) for k in offsets]
        up_own = up_for(shard_at)
        up_side = (rep_at // bits[0]) % 2
        low = up_side == 0
        up_send = [
            lax.dynamic_slice_in_dim(item, up_side * (depth // 2), depth // 2, 0) for item in up_send
        ]
        up_send, qkv_rel = lax.optimization_barrier((up_send, qkv_rel))
        up_rel = [up_own]
        for half, k in zip(up_send, offsets):
            half = turn(half, k)
            other = flip(half, bits[0])
            up_rel.append(
                jnp.concatenate([jnp.where(low, half, other), jnp.where(low, other, half)], axis=0)
            )

        small_full = jnp.concatenate(in_order(small_rel, shard_at), axis=1).astype(F32)
        out_bias_full, gain1, shift1, down_bias_full, gain2, shift2 = (
            small_full[i] for i in range(6)
        )
        came_from = (shard_at - jnp.arange(num_shard, dtype=jnp.int32)) % num_shard
        small_all = small_near + [item for pair in small_far for item in pair]

        query_mine = lax.dynamic_slice(query_bias, (core_at * att_block,), (att_block,))
        value_mine = lax.dynamic_slice(value_bias, (core_at * att_block,), (att_block,))
        qkv_bias = jnp.concatenate([query_mine, jnp.zeros_like(query_mine), value_mine]).astype(F32)
        out_mine = lax.dynamic_slice(out_weight, (core_at * att_block, 0), (att_block, width))
        down_mine = take_rows(down_weight, core_at, ff_block)
        up_bias_mine = lax.dynamic_slice(up_bias, (core_at * ff_block,), (ff_block,)).astype(F32)

        all_rows = parts * rows
        plan = (parts, num_shard, num_seqs, heads_here, head_size)
        taken = [
            came_from, *tok_near, *[item for pair in tok_far for item in pair], *small_all,
            *qkv_rel, qkv_bias.reshape(1, -1), out_mine,
        ]
        given = [
            pltpu.HBM((all_rows, width), BF16),
            pltpu.HBM((width, 3 * att_block), BF16),
            pltpu.HBM((all_rows, 3 * att_block), BF16),
            pltpu.HBM((all_rows, att_block), BF16),
        ] + [jax.ShapeDtypeStruct((rows, width), BF16)] * parts
        tok_all, qkv_mine, qkv_rows, context, *partials = pl.pallas_call(
            lambda *refs: attend_kernel(plan, *refs),
            in_specs=[SCALARS] + whole(2 * parts + num_shard + 2),
            out_specs=[pl.BlockSpec(memory_space=pltpu.HBM)] * 4 + whole(parts),
            out_shape=given,
            scratch_shapes=[pltpu.VMEM(item.shape, item.dtype) for item in given[:4]]
            + [pltpu.SemaphoreType.DMA((4,))],
            compiler_params=vmem(*taken, *given, spare=6),
            name="attend",
        )(*taken)
        resid1 = tokens.astype(F32) + scatter_rows(partials) + out_bias_full
        hidden1, normed1, inv_std1 = norm_rows(resid1, gain1, shift1)
        hid_all = stack(*gather_rows(hidden1.astype(BF16)))

        up_mine = jnp.concatenate(in_order(up_rel, shard_at), axis=0)
        pre_act = dot(hid_all, up_mine) + up_bias_mine
        activ = erf_gelu(pre_act).astype(BF16)
        slope = lax.optimization_barrier(
            gelu_slope(lax.optimization_barrier((pre_act, activ))[0]).astype(BF16)
        )
        resid2 = hidden1 + scatter_rows(split(dot(activ, down_mine).astype(BF16))) + down_bias_full
        layer_f32, normed2, inv_std2 = norm_rows(resid2, gain2, shift2)
        layer_out = layer_f32.astype(BF16)

        upstream = cotangent.astype(F32)
        grad_gain2 = jnp.sum(upstream * normed2, axis=0)
        grad_shift2 = jnp.sum(upstream, axis=0)
        grad_resid2 = norm_back(upstream, normed2, inv_std2, gain2)
        grad_down_bias = jnp.sum(grad_resid2, axis=0)
        mlp_all = stack(*gather_rows(grad_resid2.astype(BF16)))
        sum_down = dot_rows(activ, mlp_all).astype(BF16)
        grad_pre = dot_cols(mlp_all, down_mine) * slope.astype(F32)
        grad_pre_half = grad_pre.astype(BF16)
        grad_up_bias = jnp.sum(grad_pre, axis=0)
        sum_up = dot_rows(hid_all, grad_pre_half).astype(BF16)
        grad_hidden1 = grad_resid2 + scatter_rows(split(dot_cols(grad_pre_half, up_mine).astype(BF16)))
        grad_gain1 = jnp.sum(grad_hidden1 * normed1, axis=0)
        grad_shift1 = jnp.sum(grad_hidden1, axis=0)
        grad_resid1 = norm_back(grad_hidden1, normed1, inv_std1, gain1)
        grad_out_bias = jnp.sum(grad_resid1, axis=0)
        attn_near, attn_far = gather_rows(grad_resid1.astype(BF16))
        taken = [
            *attn_near, *[item for pair in attn_far for item in pair], *small_all,
            qkv_rows, out_mine,
        ]
        given = [
            jax.ShapeDtypeStruct((all_rows, width), BF16),
            jax.ShapeDtypeStruct((all_rows, 3 * att_block), BF16),
            jax.ShapeDtypeStruct((2, att_block), F32),
        ]
        attn_all, grad_qkv, bias_sums = pl.pallas_call(
            lambda *refs: attend_back_kernel(plan, *refs),
            in_specs=whole(2 * parts + 2),
            out_specs=whole(3),
            out_shape=given,
            scratch_shapes=[pltpu.VMEM((all_rows, att_block), BF16)],
            compiler_params=vmem(*taken, *given, context, spare=6),
            name="attend_back",
        )(*taken)
        sum_out = dot_rows(context, attn_all).astype(BF16)
        grad_query_bias, grad_value_bias = bias_sums[0], bias_sums[1]
        sum_qkv = dot_rows(tok_all, grad_qkv).astype(BF16)
        input_sum = scatter_rows(split(dot_cols(grad_qkv, qkv_mine).astype(BF16)))
        input_grad = (grad_resid1 + input_sum).astype(BF16)

        def side_at(route, stage):
            bit = jnp.where(core_at == 0, route[0][stage], route[1][stage])
            return (rep_at // bit) % 2

        def halve(value, axis, name):
            route = routes[name]
            for stage in range(len(bits)):
                side = side_at(route, stage)
                half = value.shape[axis] // 2
                send = lax.dynamic_slice_in_dim(value, (1 - side) * half, half, axis)
                came = step_flip(send, route, stage)
                keep = lax.dynamic_slice_in_dim(value, side * half, half, axis)
                value = (keep.astype(F32) + came.astype(F32)).astype(BF16)
            return value

        def double(value, name):
            route = backs[name]
            for stage in reversed(range(len(bits))):
                came = step_flip(value, route, stage)
                low = side_at(route, stage) == 0
                value = jnp.concatenate(
                    [jnp.where(low, value, came), jnp.where(low, came, value)], axis=0
                )
            return value

        def reduce_by_rows(value, name):
            value = double(halve(value, 0, name), name)
            other = sibling(value)
            return value, other

        def reduce_by_columns(value, repeats, name):
            piece = halve(value.reshape(num_shard, depth, -1), 1, name)
            relative = [lax.dynamic_index_in_dim(piece, shard_at, 0, keepdims=False)]
            for k in offsets:
                out_to = lax.dynamic_index_in_dim(piece, (shard_at + k) % num_shard, 0, keepdims=False)
                relative.append(turn(out_to, k))
            full = double(jnp.concatenate(in_order(relative, shard_at), axis=1), name)
            other = sibling(full)
            swap = routes[name] != backs[name]
            return merge_columns(full, other, core_at, num_shard, repeats, swap)

        total_down = merge_rows(*reduce_by_rows(sum_down, "down"), core_at)
        total_up = reduce_by_columns(sum_up, 1, "up")
        total_qkv = reduce_by_columns(sum_qkv, 3, "qkv")

        row_sums = jnp.stack(
            [grad_out_bias, grad_gain1, grad_shift1, grad_down_bias, grad_gain2, grad_shift2]
        )
        row_sums = row_sums.reshape(6, num_shard, depth)
        mine = lax.dynamic_index_in_dim(row_sums, shard_at, 1, keepdims=False)
        for k in offsets:
            there = lax.dynamic_index_in_dim(row_sums, (shard_at + k) % num_shard, 1, keepdims=False)
            mine = mine + turn(there, k)
        mine = mine + sibling(mine)
        packed = jnp.concatenate(
            [mine.reshape(-1), grad_query_bias, grad_value_bias, grad_up_bias]
        )
        beside = -(-packed.size // (128 * att_block)) * 128
        packed_rows = jnp.pad(packed, (0, att_block * beside - packed.size)).astype(BF16)
        sum_out = jnp.concatenate([sum_out, packed_rows.reshape(att_block, beside)], axis=1)
        out_here, out_there = reduce_by_rows(sum_out, "out")
        total_out = merge_rows(out_here[:, :width], out_there[:, :width], core_at)
        packed = out_here[:, width:].reshape(-1).astype(F32)
        packed_there = out_there[:, width:].reshape(-1).astype(F32)
        mine = packed[: 6 * depth].reshape(6, depth)
        block_sums = packed[6 * depth : 6 * depth + 2 * att_block + ff_block]
        other_sums = packed_there[6 * depth : 6 * depth + 2 * att_block + ff_block]
        first = jnp.where(core_at == 0, block_sums, other_sums)
        second = jnp.where(core_at == 0, other_sums, block_sums)
        total_query = jnp.concatenate([first[:att_block], second[:att_block]])
        total_value = jnp.concatenate(
            [first[att_block : 2 * att_block], second[att_block : 2 * att_block]]
        )
        total_up_bias = jnp.concatenate([first[2 * att_block :], second[2 * att_block :]])
        return (
            layer_out, input_grad, total_qkv, total_query, total_value, total_out,
            mine[0], mine[1], mine[2], total_up, total_up_bias, total_down, mine[3], mine[4], mine[5],
        )

    return on_device


def solution(mesh):
    rows, group, flat = P(("rep", "shard"), None), P("shard", None), P("shard")
    in_specs = (
        rows, P(("rep", "shard")), rows, group, flat, flat, group, flat, flat, flat,
        group, flat, group, flat, flat, flat,
    )
    out_specs = (
        rows, rows, group, flat, flat, group, flat, flat, flat, group, flat, group, flat, flat, flat,
    )
    return jax.shard_map(
        build(mesh.shape["rep"], mesh.shape["shard"]),
        mesh=mesh, in_specs=in_specs, out_specs=out_specs, check_vma=False,
    )
```
